32 devices in a mesh: grp: 2 (over y), ctx: 4 (over z), head: 2 (over x), sub: 2 (over core).
Axes of the slice: x: 2, y: 2, z: 4, core: 2. Of those that a mesh axis runs over, the one named last changes fastest.
Arguments:
- queries: bfloat16 [512, 16384], P(('grp', 'ctx', 'head', 'sub')), parts along dimension 0, may hold values from -400 to 400
- kv_cache: bfloat16 [2, 8192, 1024], P(None, ('grp', 'ctx', 'sub'), 'head'), parts along dimension 1, may hold values from -6 to 6
- page_counts: int32 [8], P('grp'), parts along dimension 0, may hold values from 1 to 4, as said below
Outputs:
- attended: bfloat16 [512, 16384], P(('grp', 'ctx', 'head', 'sub')), parts along dimension 0
The draws below stay inside these ranges and needn't reach their ends.
There are 2 independent parts, one for each index of `grp`. The reference program is written for one: setup_inputs(seed, part) draws one part's arguments, and reference() takes and returns one part's arrays. A program takes and returns all parts, laid end to end along the dimension named above; each array names one. Nothing has to cross between parts.
Inputs may be any that keep to these rules, and one draw needn't show every extreme that they name: `page_counts`: each count is at least 1, the counts sum to exactly 8, and one request has exactly 4 pages.
All inputs are finite; a program needn't handle non-finite values.
Results may differ from the reference program's by a relative error of at most 0.014.
Values may be sent and summed in bfloat16 or wider, within the bound.
A program may use at most 64 MiB of HBM per device.

```python
import jax
import jax.numpy as jnp
from jax import lax

HQ = 128
KVH = 8
HD = 128
REQS = 4
QR = 64
PAGE = 256
SPAN = 256
CTX = 4096
LIVE_PAGES = 8


def page_split(key):
    largest = LIVE_PAGES // 2
    first_key, second_key, shuffle_key = jax.random.split(jax.random.fold_in(key, 11), 3)
    first_cut = jax.random.randint(first_key, (), 1, largest - 1)
    second_cut = jax.random.randint(second_key, (), 1, largest - first_cut)
    counts = jnp.stack([jnp.int32(largest), first_cut, second_cut, largest - first_cut - second_cut]).astype(jnp.int32)
    shuffle = jax.random.permutation(shuffle_key, REQS)
    return counts[shuffle]


def cache_field(key):
    field_values = jax.random.normal(jax.random.fold_in(key, 23), (2, CTX, KVH * HD), jnp.float32)
    field_values = jnp.clip(field_values, -6.0, 6.0)
    return field_values


def draw_page_counts(key, part):
    return page_split(key)


def draw_kv_cache(key, part):
    return cache_field(key).astype(jnp.bfloat16)


def draw_queries(key, part):
    drawn = jax.random.normal(jax.random.fold_in(key, 37), (SPAN, HQ * HD), jnp.float32)
    field_values = 2.5 * jnp.clip(drawn, -6.0, 6.0)
    return field_values.astype(jnp.bfloat16)


def setup_inputs(seed: int = 0, part: int = 0) -> dict:
    streams_of = jax.random.split(jax.random.key(seed), 4)
    own_keys = jax.random.split(jax.random.fold_in(streams_of[3], part), 4)
    return {
        "queries": draw_queries(jax.random.fold_in(jax.random.fold_in(streams_of[3], part), 71), part),
        "kv_cache": draw_kv_cache(jax.random.fold_in(jax.random.fold_in(streams_of[3], part), 71), part),
        "page_counts": draw_page_counts(jax.random.fold_in(jax.random.fold_in(streams_of[3], part), 71), part),
    }


NEG = -1e30


def reference(queries, kv_cache, page_counts):
    per_group = HQ // KVH
    live = LIVE_PAGES * PAGE
    base = CTX - live
    page_ends = jnp.cumsum(page_counts).astype(jnp.int32) * PAGE
    page_starts = page_ends - page_counts.astype(jnp.int32) * PAGE
    cache_keys = kv_cache[0, base:].astype(jnp.float32).reshape(live, KVH, HD)
    cache_values = kv_cache[1, base:].astype(jnp.float32).reshape(live, KVH, HD)
    grouped = queries.astype(jnp.float32).reshape(REQS, QR, KVH, per_group, HD)
    places = jnp.arange(live, dtype=jnp.int32)
    offsets = jnp.arange(QR, dtype=jnp.int32)
    score_scale = HD ** -0.5

    def one_request(request):
        query_pos = page_ends[request] - QR + offsets
        visible = (places[None, :] >= page_starts[request]) & (places[None, :] <= query_pos[:, None])
        request_rows = grouped[request]

        def one_head(head_id):
            query_head = request_rows[:, head_id]
            key_head = cache_keys[:, head_id]
            value_head = cache_values[:, head_id]
            scores = jnp.einsum('qgd,pd->qgp', query_head, key_head) * score_scale
            scores = jnp.where(visible[:, None, :], scores, NEG)
            top_score = jnp.max(scores, axis=2, keepdims=True)
            numerators = jnp.exp(scores - top_score)
            totals = jnp.sum(numerators, axis=2)
            weights = numerators.astype(jnp.bfloat16).astype(jnp.float32)
            return jnp.einsum('qgp,pd->qgd', weights, value_head) / totals[..., None]

        heads_out = lax.map(one_head, jnp.arange(KVH, dtype=jnp.int32))
        return jnp.transpose(heads_out, (1, 0, 2, 3))

    result = lax.map(one_request, jnp.arange(REQS, dtype=jnp.int32))
    return result.reshape(SPAN, HQ * HD).astype(jnp.bfloat16)
```

```python
import functools
import math

import jax
import jax.numpy as jnp
from jax import lax
from jax.experimental import pallas as pl
from jax.experimental.pallas import tpu as pltpu
from jax.sharding import PartitionSpec as P

HQ = 128
KVH = 8
HD = 128
REQS = 4
QR = 64
PAGE = 256
SPAN = 256


NEG = -1e30
MESH = pl.DeviceIdType.MESH
VMEM_LIMIT = 67043328


def from_behind(array, axis, by):
    count = lax.axis_size(axis)
    pairs = [(i, i + by) for i in range(count) if 0 <= i + by < count]
    return lax.ppermute(array, axis, pairs)


def per_device(queries, kv_cache, page_counts):
    per_group = HQ // KVH
    local_heads = kv_cache.shape[2] // HD
    ctx_size = lax.axis_size("ctx")
    sub_size = lax.axis_size("sub")
    head_count = lax.axis_size("head")
    tok_rows = queries.shape[0]
    score_scale = HD ** (-0.5)
    regrouped = lax.all_to_all(queries, "head", split_axis=1, concat_axis=0, tiled=True)
    all_queries = lax.all_gather(regrouped, ("ctx", "sub"), axis=0, tiled=True)
    all_queries = all_queries.reshape(SPAN, local_heads, per_group, HD)
    page_ends = jnp.cumsum(page_counts)
    ctx_rows = SPAN // ctx_size
    offsets = jnp.arange(QR, dtype=jnp.int32)
    columns = jnp.arange(PAGE, dtype=jnp.int32)
    flat_index = lax.axis_index("ctx") * sub_size + lax.axis_index("sub")
    pages_here = kv_cache.shape[1] // PAGE
    base_pages = pages_here * ctx_size * sub_size // 2
    initial = (
        jnp.full((SPAN, local_heads, per_group), NEG, jnp.float32),
        jnp.zeros((SPAN, local_heads, per_group), jnp.float32),
        jnp.zeros((SPAN, local_heads, per_group, HD), jnp.float32),
    )
    half_rows = kv_cache.shape[1] // 2
    arrived = from_behind(kv_cache[:, half_rows:], "ctx", -(ctx_size // 2))
    is_lower = lax.axis_index("ctx") < ctx_size // 2
    source_flat = flat_index + ctx_size // 2 * sub_size
    working = jnp.where(is_lower, arrived, kv_cache[:, :half_rows])
    first_page = jnp.where(
        is_lower, source_flat * pages_here + pages_here // 2, flat_index * pages_here
    )
    page_total = working.shape[1] // PAGE

    def add_page(page_turn, running):
        page_index = first_page + page_turn
        relative = page_index - base_pages
        counted = jnp.sum((relative >= page_ends).astype(jnp.int32))
        request = jnp.where(relative < 0, REQS, counted)

        def update(partial_value):
            run_max, run_sum, run_out = partial_value
            request_id = jnp.minimum(request, REQS - 1)
            row_start = request_id * QR
            gathered = row_start + offsets
            within = gathered % ctx_rows
            ctx_block = gathered // ctx_rows
            sub_part = within // (head_count * tok_rows)
            head_part = within // tok_rows % head_count
            tok_part = within % tok_rows
            natural = ctx_block * ctx_rows + (head_part * sub_size + sub_part) * tok_rows + tok_part
            query_pos = (page_ends[request_id] + base_pages) * PAGE - QR + natural - row_start
            key_pos = page_index * PAGE + columns
            visible = key_pos[None, :] <= query_pos[:, None]
            page_keys = working[0].reshape(PAGE, local_heads, HD)
            page_values = working[1].reshape(PAGE, local_heads, HD)
            query_rows = lax.dynamic_slice_in_dim(all_queries, row_start, QR, 0)
            scores = (
                jnp.einsum(
                    "qkgd,pkd->qkgp", query_rows, page_keys, preferred_element_type=jnp.float32
                )
                * score_scale
            )
            scores = jnp.where(visible[:, None, None, :], scores, NEG)
            old_max = lax.dynamic_slice_in_dim(run_max, row_start, QR, 0)
            old_sum = lax.dynamic_slice_in_dim(run_sum, row_start, QR, 0)
            old_out = lax.dynamic_slice_in_dim(run_out, row_start, QR, 0)
            new_max = jnp.maximum(old_max, jnp.max(scores, axis=3))
            factor = jnp.exp(old_max - new_max)
            numerators = jnp.exp(scores - new_max[..., None])
            new_sum = old_sum * factor + jnp.sum(numerators, axis=3)
            product = jnp.einsum(
                "qkgp,pkd->qkgd",
                numerators.astype(jnp.bfloat16),
                page_values,
                preferred_element_type=jnp.float32,
            )
            new_out = old_out * factor[..., None] + product
            return (
                lax.dynamic_update_slice_in_dim(run_max, new_max, row_start, 0),
                lax.dynamic_update_slice_in_dim(run_sum, new_sum, row_start, 0),
                lax.dynamic_update_slice_in_dim(run_out, new_out, row_start, 0),
            )

        def unchanged(partial_value):
            return partial_value

        return lax.cond(request < REQS, update, unchanged, running)

    run_max, run_sum, run_out = lax.fori_loop(0, page_total, add_page, initial)
    share = SPAN // (ctx_size * sub_size)
    global_max = lax.pmax(run_max, ("ctx", "sub"))
    factor = jnp.exp(run_max - global_max)
    sums_here, outs_here = (
        lax.psum_scatter(
            (run_sum * factor).astype(jnp.bfloat16), ("ctx", "sub"), scatter_dimension=0, tiled=True
        ).astype(jnp.float32),
        lax.psum_scatter(
            (run_out * factor[..., None]).astype(jnp.bfloat16),
            ("ctx", "sub"),
            scatter_dimension=0,
            tiled=True,
        ).astype(jnp.float32),
    )
    finished = (outs_here / sums_here[..., None]).astype(jnp.bfloat16)
    finished = finished.reshape(share, local_heads * per_group * HD)
    return lax.all_to_all(finished, "head", split_axis=0, concat_axis=1, tiled=True)


FAR, NEAR, HUB, TOP = range(4)


def can_serve(mesh, rows):
    ctx_size, sub_size, head_size = mesh.shape["ctx"], mesh.shape["sub"], mesh.shape["head"]
    if ctx_size != REQS or SPAN // ctx_size != QR or sub_size != 2:
        return False
    pages_here = rows // (mesh.shape["grp"] * ctx_size * sub_size) // PAGE
    return pages_here == 2 and KVH == 2 * head_size * sub_size


def serve_kernel(
    sizes,
    counts_ref,
    q_hbm,
    kv_hbm,
    out_ref,
    kvbuf,
    qbuf,
    obuf,
    sbuf,
    q_send,
    q_recv,
    o_send,
    o_recv,
    kv_send,
    kv_recv,
    go,
):
    head_size, sub_size, pages_here = sizes
    mates = head_size * sub_size
    per_core = KVH // mates
    group = HQ // KVH
    width = group * HD
    tok_rows = QR // mates
    rows = group * tok_rows
    split = pages_here * sub_size
    live = 2 * split
    z, x, s = lax.axis_index("ctx"), lax.axis_index("head"), lax.axis_index("sub")
    mine = x * sub_size + s
    slot_of = jnp.minimum(z, HUB)
    factor = HD ** (-0.5) * math.log2(math.e)

    def at(device, plane=None):
        place = {"head": device // sub_size, "sub": device % sub_size}
        if plane is not None:
            place["ctx"] = plane
        return place

    barrier = pltpu.get_barrier_semaphore()

    def greet(place):
        pl.semaphore_signal(barrier, device_id=place, device_id_type=MESH)

    def greet_plane(plane):
        for device in range(mates):
            greet(at(device, plane))

    def greet_mates():
        for step in range(1, mates):
            greet(at(lax.rem(mine + step, mates)))

    @pl.when(z == HUB)
    def _():
        greet_plane(NEAR)
        greet_plane(FAR)
        greet_mates()
        for core in range(sub_size):
            greet({"ctx": TOP, "sub": core})
        pl.semaphore_wait(barrier, 3 * mates - 1)

    @pl.when(z == TOP)
    def _():
        greet_mates()
        pl.semaphore_wait(barrier, mates - 1 + sub_size)

    @pl.when(z == NEAR)
    def _():
        greet_plane(HUB)
        greet({"ctx": FAR})
        pl.semaphore_wait(barrier, mates)

    @pl.when(z == FAR)
    def _():
        greet_plane(HUB)
        greet_mates()
        pl.semaphore_wait(barrier, 2 * mates)

    def cols(device, h):
        return pl.ds(pl.multiple_of((device * per_core + h) * width, width), width)

    def q_remote(h, step, plane):
        other = lax.rem(mine + step, mates)
        return pltpu.make_async_remote_copy(
            src_ref=q_hbm.at[:, cols(other, h)],
            dst_ref=qbuf.at[slot_of, h, mine],
            send_sem=q_send.at[h, step],
            recv_sem=q_recv.at[slot_of, h, mine],
            device_id=at(other, plane),
            device_id_type=MESH,
        )

    def q_local(h):
        return pltpu.make_async_copy(
            q_hbm.at[:, cols(mine, h)], qbuf.at[slot_of, h, mine], q_recv.at[slot_of, h, mine]
        )

    def q_await(slot, h, device):
        pltpu.make_async_copy(
            q_hbm.at[:, cols(0, 0)], qbuf.at[slot, h, device], q_recv.at[slot, h, device]
        ).wait()

    def o_remote(slot, h, device, plane):
        return pltpu.make_async_remote_copy(
            src_ref=obuf.at[slot, h, device],
            dst_ref=out_ref.at[:, cols(mine, h)],
            send_sem=o_send.at[slot, h, device],
            recv_sem=o_recv.at[h, mine],
            device_id=at(device, plane),
            device_id_type=MESH,
        )

    def o_local(slot, h):
        return pltpu.make_async_copy(
            obuf.at[slot, h, mine], out_ref.at[:, cols(mine, h)], o_recv.at[h, mine]
        )

    def kv_block(k, local, core, h):
        return kv_hbm.at[
            k,
            pl.ds(local * PAGE, PAGE),
            pl.ds(pl.multiple_of((core * per_core + h) * HD, HD), HD),
        ]

    def kv_place(h, k, p):
        return kvbuf.at[h, k, pl.ds(pl.multiple_of(p * PAGE, PAGE), PAGE)]

    def kv_remote(kind, h, k, local, p, core, target):
        return pltpu.make_async_remote_copy(
            src_ref=kv_block(k, local, core, h),
            dst_ref=kv_place(h, k, p),
            send_sem=kv_send.at[kind, h, k, local],
            recv_sem=kv_recv.at[h, k, p],
            device_id=target,
            device_id_type=MESH,
        )

    def kv_local(h, k, local, p):
        return pltpu.make_async_copy(
            kv_block(k, local, s, h), kv_place(h, k, p), kv_recv.at[h, k, p]
        )

    def kv_await(h, pages):
        for k in range(2):
            for p in pages:
                pltpu.make_async_copy(
                    kv_block(0, 0, 0, 0), kv_place(h, k, p), kv_recv.at[h, k, p]
                ).wait()

    def first_local():
        return (s + jnp.where(z == TOP, sub_size, 0)) * pages_here

    def exchange(act, local_act):
        first = first_local()
        for h in range(per_core):
            for k in range(2):
                for local in range(pages_here):
                    act(kv_remote(0, h, k, local, first + local, 1 - s, {"sub": 1 - s}))
                    if local_act is not None:
                        local_act(kv_local(h, k, local, first + local))

    def hand_far(act):
        h = per_core - 1
        for k in range(2):
            for local in range(pages_here):
                act(
                    kv_remote(
                        1, h, k, local, first_local() + local, sub_size - 1,
                        {"ctx": FAR, "sub": sub_size - 1},
                    )
                )

    def hand_hub(act, held):
        for h in range(per_core):
            for core in range(sub_size):
                for k in range(2):
                    for local in range(held):
                        act(
                            kv_remote(
                                1 + core, h, k, local, first_local() + local, core,
                                {"ctx": HUB, "sub": core},
                            )
                        )

    def start(copy):
        copy.start()

    def sent(copy):
        copy.wait_send()

    def span_of(r):
        first, count = jnp.int32(0), jnp.int32(0)
        for i in range(REQS):
            if i < r:
                first = first + counts_ref[i]
            if i == r:
                count = counts_ref[i]
        return first * PAGE, (first + count) * PAGE - QR

    token = lax.broadcasted_iota(jnp.int32, (tok_rows, PAGE), 0)
    column = lax.broadcasted_iota(jnp.int32, (tok_rows, PAGE), 1)

    def attend(slot, h, device, pages, span):
        first_pos, query_base = span
        last_seen = query_base + device * tok_rows + token
        query = jnp.concatenate(
            [qbuf[slot, h, device, :, j * HD : (j + 1) * HD] for j in range(group)], axis=0
        )
        top = jnp.full((rows, HD), NEG, jnp.float32)
        for n, p in enumerate(pages):
            keys = kvbuf[h, 0, p * PAGE : (p + 1) * PAGE, :]
            pos = p * PAGE + column
            bias = jnp.where((pos >= first_pos) & (pos <= last_seen), 0.0, NEG)
            scores = lax.dot_general(
                query, keys, (((1,), (1,)), ((), ())), preferred_element_type=jnp.float32
            )
            scores = scores.reshape(group, tok_rows, PAGE) + bias[None]
            scores = scores.reshape(rows, PAGE)
            sbuf[:, n * PAGE : (n + 1) * PAGE] = scores
            for c in range(PAGE // HD):
                top = jnp.maximum(top, scores[:, c * HD : (c + 1) * HD])
        top = jnp.broadcast_to(jnp.max(top, axis=1, keepdims=True), (rows, HD))
        total = jnp.zeros((rows, HD), jnp.float32)
        summed = jnp.zeros((rows, HD), jnp.float32)
        for n, p in enumerate(pages):
            parts = []
            for c in range(PAGE // HD):
                low = n * PAGE + c * HD
                parts.append(jnp.exp2((sbuf[:, low : low + HD] - top) * factor))
                total = total + parts[-1]
            weights = jnp.concatenate([part.astype(jnp.bfloat16) for part in parts], axis=1)
            values = kvbuf[h, 1, p * PAGE : (p + 1) * PAGE, :]
            summed = summed + jnp.dot(weights, values, preferred_element_type=jnp.float32)
        done = summed / jnp.sum(total, axis=1, keepdims=True)
        done = done.astype(jnp.bfloat16)
        for j in range(group):
            obuf[slot, h, device, :, j * HD : (j + 1) * HD] = done[
                j * tok_rows : (j + 1) * tok_rows, :
            ]

    def turn(slot, h, i, pages, span, plane, own):
        device = lax.rem(mine - i + mates, mates)
        q_await(slot, h, device)
        attend(slot, h, device, pages, span)
        stays = own & (i == 0)

        @pl.when(stays)
        def _():
            o_local(slot, h).start()

        @pl.when(jnp.logical_not(stays))
        def _():
            o_remote(slot, h, device, plane).start()

    far_pages = range(split)
    near_pages = range(1, live - 2)
    hub_pages = range(2, live - 1)
    top_pages = range(split, live)
    last = per_core - 1

    def stays_far(h, step):
        return (h == last) & (lax.rem(s + step, sub_size) == sub_size - 1)

    @pl.when(z == HUB)
    def _():
        hand_far(start)
        exchange(start, start)

    @pl.when((z == TOP) & (s == 0))
    def _():
        hand_hub(start, pages_here)

    @pl.when(z == TOP)
    def _():
        exchange(start, start)

    @pl.when(z >= HUB)
    def _():
        for h in range(per_core):
            q_local(h).start()
            for step in range(1, mates):
                q_remote(h, step, z).start()

    @pl.when(z == FAR)
    def _():
        for h in range(per_core):
            for step in range(mates):
                if h < last:
                    q_remote(h, step, HUB).start()
                else:
                    keep = stays_far(h, step)

                    @pl.when(jnp.logical_not(keep))
                    def _():
                        q_remote(h, step, HUB).start()

                    @pl.when(keep)
                    def _():
                        if step:
                            q_remote(h, step, FAR).start()
                        else:
                            q_local(h).start()

        for h in range(last):
            for step in range(mates):
                q_remote(h, step, HUB).wait_send()
        pl.semaphore_signal(go, device_id={"ctx": NEAR}, device_id_type=MESH)

    @pl.when(z == NEAR)
    def _():
        pl.semaphore_wait(go, 1)
        for h in range(per_core):
            for step in range(mates):
                q_remote(h, step, HUB).start()

    @pl.when((z == HUB) | ((z == FAR) & (s == sub_size - 1)))
    def _():
        span = span_of(FAR)
        h_low = jnp.where(z == FAR, last, 0)
        h_high = jnp.where((z == HUB) & (s == sub_size - 1), last, per_core)

        def step(n, carry):
            h, i = n // mates, n % mates

            @pl.when(i == 0)
            def _():
                kv_await(h, far_pages)

            turn(FAR, h, i, far_pages, span, FAR, z == FAR)
            return carry

        lax.fori_loop(h_low * mates, h_high * mates, step, 0)

    @pl.when(z == HUB)
    def _():
        @pl.when(s == sub_size - 1)
        def _():
            kv_await(last, far_pages)

        near_span, hub_span = span_of(NEAR), span_of(HUB)

        def head_turn(h, carry):
            kv_await(h, [p for p in near_pages if p >= split])

            def near(i, carry):
                turn(NEAR, h, i, near_pages, near_span, NEAR, False)
                return carry

            lax.fori_loop(0, mates, near, 0)
            kv_await(h, [p for p in hub_pages if p >= split and p not in near_pages])

            def own(i, carry):
                turn(HUB, h, i, hub_pages, hub_span, HUB, True)
                return carry

            lax.fori_loop(0, mates, own, 0)
            return carry

        lax.fori_loop(0, per_core, head_turn, 0)

    @pl.when(z == TOP)
    def _():
        span = span_of(TOP)

        def step(n, carry):
            h, i = n // mates, n % mates

            @pl.when(i == 0)
            def _():
                kv_await(h, top_pages)

            turn(HUB, h, i, top_pages, span, TOP, True)
            return carry

        lax.fori_loop(0, per_core * mates, step, 0)

        @pl.when(s == 0)
        def _():
            hand_hub(sent, pages_here)
            pl.semaphore_signal(go, device_id={"sub": 1}, device_id_type=MESH)

        @pl.when(s == 1)
        def _():
            pl.semaphore_wait(go, 1)
            hand_hub(start, 1)
            hand_hub(sent, 1)

    for h in range(per_core):
        for device in range(mates):
            pltpu.make_async_copy(
                obuf.at[0, 0, 0], out_ref.at[:, cols(device, h)], o_recv.at[h, device]
            ).wait()

    @pl.when(z == HUB)
    def _():
        hand_far(sent)

        def drain(n, carry):
            h, device = n // mates, n % mates
            o_remote(NEAR, h, device, NEAR).wait_send()
            return carry

        lax.fori_loop(0, per_core * mates, drain, 0)

    @pl.when((z == HUB) | ((z == FAR) & (s == sub_size - 1)))
    def _():
        h_low = jnp.where(z == FAR, last, 0)
        h_high = jnp.where((z == HUB) & (s == sub_size - 1), last, per_core)

        def drain(n, carry):
            h, i = n // mates, n % mates

            @pl.when((z == HUB) | (i > 0))
            def _():
                o_remote(FAR, h, lax.rem(mine - i + mates, mates), FAR).wait_send()

            return carry

        lax.fori_loop(h_low * mates, h_high * mates, drain, 0)

    @pl.when(z >= HUB)
    def _():
        exchange(sent, None)
        for h in range(per_core):
            for step in range(1, mates):
                q_remote(h, step, z).wait_send()
                o_remote(HUB, h, lax.rem(mine + step, mates), z).wait_send()

    @pl.when(z == NEAR)
    def _():
        for h in range(per_core):
            for step in range(mates):
                q_remote(h, step, HUB).wait_send()

    @pl.when(z == FAR)
    def _():
        for step in range(mates):
            if step:
                q_remote(last, step, HUB).wait_send()
            else:
                @pl.when(jnp.logical_not(stays_far(last, step)))
                def _():
                    q_remote(last, step, HUB).wait_send()


def served(queries, kv_cache, page_counts):
    ctx_size, sub_size = lax.axis_size("ctx"), lax.axis_size("sub")
    head_size = lax.axis_size("head")
    pages_here = kv_cache.shape[1] // PAGE
    mates = head_size * sub_size
    per_core = KVH // mates
    group = HQ // KVH
    live = pages_here * ctx_size * sub_size // 2
    tok_rows = queries.shape[0]
    slots = ctx_size - 1
    dma = pltpu.SemaphoreType.DMA
    chunk = (slots, per_core, mates, tok_rows, group * HD)
    return pl.pallas_call(
        functools.partial(serve_kernel, (head_size, sub_size, pages_here)),
        out_shape=jax.ShapeDtypeStruct(queries.shape, jnp.bfloat16),
        in_specs=[
            pl.BlockSpec(memory_space=pltpu.SMEM),
            pl.BlockSpec(memory_space=pl.ANY),
            pl.BlockSpec(memory_space=pl.ANY),
        ],
        out_specs=pl.BlockSpec(memory_space=pl.ANY),
        scratch_shapes=[
            pltpu.VMEM((per_core, 2, live * PAGE, HD), jnp.bfloat16),
            pltpu.VMEM(chunk, jnp.bfloat16),
            pltpu.VMEM(chunk, jnp.bfloat16),
            pltpu.VMEM((group * tok_rows, (live - 3) * PAGE), jnp.float32),
            dma((per_core, mates)),
            dma((slots, per_core, mates)),
            dma((slots, per_core, mates)),
            dma((per_core, mates)),
            dma((1 + sub_size, per_core, 2, pages_here)),
            dma((per_core, 2, live)),
            pltpu.SemaphoreType.REGULAR,
        ],
        compiler_params=pltpu.CompilerParams(
            collective_id=0, has_side_effects=True, vmem_limit_bytes=VMEM_LIMIT
        ),
    )(page_counts, queries, kv_cache)


def solution(mesh):
    specs = dict(
        mesh=mesh,
        in_specs=(
            P(("grp", "ctx", "head", "sub"), None),
            P(None, ("grp", "ctx", "sub"), "head"),
            P("grp"),
        ),
        out_specs=P(("grp", "ctx", "head", "sub"), None),
        check_vma=False,
    )

    def run(queries, kv_cache, page_counts):
        body = served if can_serve(mesh, kv_cache.shape[1]) else per_device
        return jax.shard_map(body, **specs)(queries, kv_cache, page_counts)

    return run
```

```python
import functools
import math

import jax
import jax.numpy as jnp
from jax import lax
from jax.experimental import pallas as pl
from jax.experimental.pallas import tpu as pltpu
from jax.sharding import PartitionSpec as P

HQ = 128
KVH = 8
HD = 128
REQS = 4
QR = 64
PAGE = 256
SPAN = 256


NEG = -1e30
MESH = pl.DeviceIdType.MESH
VMEM_LIMIT = 40000000
EARLY = 1
AHEAD = 3


def from_behind(array, axis, by):
    count = lax.axis_size(axis)
    pairs = [(i, i + by) for i in range(count) if 0 <= i + by < count]
    return lax.ppermute(array, axis, pairs)


def per_device(queries, kv_cache, page_counts):
    per_group = HQ // KVH
    local_heads = kv_cache.shape[2] // HD
    ctx_size = lax.axis_size("ctx")
    sub_size = lax.axis_size("sub")
    head_count = lax.axis_size("head")
    tok_rows = queries.shape[0]
    score_scale = HD ** (-0.5)
    regrouped = lax.all_to_all(queries, "head", split_axis=1, concat_axis=0, tiled=True)
    all_queries = lax.all_gather(regrouped, ("ctx", "sub"), axis=0, tiled=True)
    all_queries = all_queries.reshape(SPAN, local_heads, per_group, HD)
    page_ends = jnp.cumsum(page_counts)
    ctx_rows = SPAN // ctx_size
    offsets = jnp.arange(QR, dtype=jnp.int32)
    columns = jnp.arange(PAGE, dtype=jnp.int32)
    flat_index = lax.axis_index("ctx") * sub_size + lax.axis_index("sub")
    pages_here = kv_cache.shape[1] // PAGE
    base_pages = pages_here * ctx_size * sub_size // 2
    initial = (
        jnp.full((SPAN, local_heads, per_group), NEG, jnp.float32),
        jnp.zeros((SPAN, local_heads, per_group), jnp.float32),
        jnp.zeros((SPAN, local_heads, per_group, HD), jnp.float32),
    )
    half_rows = kv_cache.shape[1] // 2
    arrived = from_behind(kv_cache[:, half_rows:], "ctx", -(ctx_size // 2))
    is_lower = lax.axis_index("ctx") < ctx_size // 2
    source_flat = flat_index + ctx_size // 2 * sub_size
    working = jnp.where(is_lower, arrived, kv_cache[:, :half_rows])
    first_page = jnp.where(
        is_lower, source_flat * pages_here + pages_here // 2, flat_index * pages_here
    )
    page_total = working.shape[1] // PAGE

    def add_page(page_turn, running):
        page_index = first_page + page_turn
        relative = page_index - base_pages
        counted = jnp.sum((relative >= page_ends).astype(jnp.int32))
        request = jnp.where(relative < 0, REQS, counted)

        def update(partial_value):
            run_max, run_sum, run_out = partial_value
            request_id = jnp.minimum(request, REQS - 1)
            row_start = request_id * QR
            gathered = row_start + offsets
            within = gathered % ctx_rows
            ctx_block = gathered // ctx_rows
            sub_part = within // (head_count * tok_rows)
            head_part = within // tok_rows % head_count
            tok_part = within % tok_rows
            natural = ctx_block * ctx_rows + (head_part * sub_size + sub_part) * tok_rows + tok_part
            query_pos = (page_ends[request_id] + base_pages) * PAGE - QR + natural - row_start
            key_pos = page_index * PAGE + columns
            visible = key_pos[None, :] <= query_pos[:, None]
            page_keys = working[0].reshape(PAGE, local_heads, HD)
            page_values = working[1].reshape(PAGE, local_heads, HD)
            query_rows = lax.dynamic_slice_in_dim(all_queries, row_start, QR, 0)
            scores = (
                jnp.einsum(
                    "qkgd,pkd->qkgp", query_rows, page_keys, preferred_element_type=jnp.float32
                )
                * score_scale
            )
            scores = jnp.where(visible[:, None, None, :], scores, NEG)
            old_max = lax.dynamic_slice_in_dim(run_max, row_start, QR, 0)
            old_sum = lax.dynamic_slice_in_dim(run_sum, row_start, QR, 0)
            old_out = lax.dynamic_slice_in_dim(run_out, row_start, QR, 0)
            new_max = jnp.maximum(old_max, jnp.max(scores, axis=3))
            factor = jnp.exp(old_max - new_max)
            numerators = jnp.exp(scores - new_max[..., None])
            new_sum = old_sum * factor + jnp.sum(numerators, axis=3)
            product = jnp.einsum(
                "qkgp,pkd->qkgd",
                numerators.astype(jnp.bfloat16),
                page_values,
                preferred_element_type=jnp.float32,
            )
            new_out = old_out * factor[..., None] + product
            return (
                lax.dynamic_update_slice_in_dim(run_max, new_max, row_start, 0),
                lax.dynamic_update_slice_in_dim(run_sum, new_sum, row_start, 0),
                lax.dynamic_update_slice_in_dim(run_out, new_out, row_start, 0),
            )

        def unchanged(partial_value):
            return partial_value

        return lax.cond(request < REQS, update, unchanged, running)

    run_max, run_sum, run_out = lax.fori_loop(0, page_total, add_page, initial)
    share = SPAN // (ctx_size * sub_size)
    global_max = lax.pmax(run_max, ("ctx", "sub"))
    factor = jnp.exp(run_max - global_max)
    sums_here, outs_here = (
        lax.psum_scatter(
            (run_sum * factor).astype(jnp.bfloat16), ("ctx", "sub"), scatter_dimension=0, tiled=True
        ).astype(jnp.float32),
        lax.psum_scatter(
            (run_out * factor[..., None]).astype(jnp.bfloat16),
            ("ctx", "sub"),
            scatter_dimension=0,
            tiled=True,
        ).astype(jnp.float32),
    )
    finished = (outs_here / sums_here[..., None]).astype(jnp.bfloat16)
    finished = finished.reshape(share, local_heads * per_group * HD)
    return lax.all_to_all(finished, "head", split_axis=0, concat_axis=1, tiled=True)


FAR, NEAR, HUB, TOP = range(4)


def can_serve(mesh, rows):
    ctx_size, sub_size, head_size = mesh.shape["ctx"], mesh.shape["sub"], mesh.shape["head"]
    if ctx_size != REQS or SPAN // ctx_size != QR or sub_size != 2:
        return False
    pages_here = rows // (mesh.shape["grp"] * ctx_size * sub_size) // PAGE
    return pages_here == 2 and KVH == 2 * head_size * sub_size


def serve_kernel(
    sizes,
    counts_ref,
    q_hbm,
    kv_hbm,
    out_ref,
    kvbuf,
    qbuf,
    obuf,
    sbuf,
    tbuf,
    q_send,
    q_recv,
    o_send,
    o_recv,
    kv_send,
    kv_recv,
    go,
):
    head_size, sub_size, pages_here = sizes
    mates = head_size * sub_size
    per_core = KVH // mates
    group = HQ // KVH
    width = group * HD
    tok_rows = QR // mates
    rows = group * tok_rows
    split = pages_here * sub_size
    live = 2 * split
    z, x, s = lax.axis_index("ctx"), lax.axis_index("head"), lax.axis_index("sub")
    mine = x * sub_size + s
    slot_of = jnp.minimum(z, HUB)
    factor = HD ** (-0.5) * math.log2(math.e)

    def at(device, plane=None):
        place = {"head": device // sub_size, "sub": device % sub_size}
        if plane is not None:
            place["ctx"] = plane
        return place

    barrier = pltpu.get_barrier_semaphore()

    def greet(place):
        pl.semaphore_signal(barrier, device_id=place, device_id_type=MESH)

    def greet_plane(plane):
        for device in range(mates):
            greet(at(device, plane))

    def greet_mates():
        for step in range(1, mates):
            greet(at(lax.rem(mine + step, mates)))

    @pl.when(z == HUB)
    def _():
        greet_plane(NEAR)
        greet_plane(FAR)
        greet_mates()
        for core in range(sub_size):
            greet({"ctx": TOP, "sub": core})
        pl.semaphore_wait(barrier, 3 * mates - 1)

    @pl.when(z == TOP)
    def _():
        greet_mates()
        pl.semaphore_wait(barrier, mates - 1 + sub_size)

    @pl.when(z == NEAR)
    def _():
        greet_plane(HUB)
        greet({"ctx": FAR})
        pl.semaphore_wait(barrier, mates)

    @pl.when(z == FAR)
    def _():
        greet_plane(HUB)
        greet_mates()
        pl.semaphore_wait(barrier, 2 * mates)

    def cols(device, h):
        return pl.ds(pl.multiple_of((device * per_core + h) * width, width), width)

    def q_remote(h, step, plane):
        other = lax.rem(mine + step, mates)
        return pltpu.make_async_remote_copy(
            src_ref=q_hbm.at[:, cols(other, h)],
            dst_ref=qbuf.at[slot_of, h, mine],
            send_sem=q_send.at[h, step],
            recv_sem=q_recv.at[slot_of, h, mine],
            device_id=at(other, plane),
            device_id_type=MESH,
        )

    def q_local(h):
        return pltpu.make_async_copy(
            q_hbm.at[:, cols(mine, h)], qbuf.at[slot_of, h, mine], q_recv.at[slot_of, h, mine]
        )

    def q_await(slot, h, device):
        pltpu.make_async_copy(
            q_hbm.at[:, cols(0, 0)], qbuf.at[slot, h, device], q_recv.at[slot, h, device]
        ).wait()

    def o_remote(slot, h, device, plane):
        return pltpu.make_async_remote_copy(
            src_ref=obuf.at[slot, h, device],
            dst_ref=out_ref.at[:, cols(mine, h)],
            send_sem=o_send.at[slot, h, device],
            recv_sem=o_recv.at[h, mine],
            device_id=at(device, plane),
            device_id_type=MESH,
        )

    def o_local(slot, h):
        return pltpu.make_async_copy(
            obuf.at[slot, h, mine], out_ref.at[:, cols(mine, h)], o_recv.at[h, mine]
        )

    def kv_block(k, local, core, h):
        return kv_hbm.at[
            k,
            pl.ds(local * PAGE, PAGE),
            pl.ds(pl.multiple_of((core * per_core + h) * HD, HD), HD),
        ]

    def kv_place(h, k, p):
        return kvbuf.at[h, k, pl.ds(pl.multiple_of(p * PAGE, PAGE), PAGE)]

    def kv_remote(kind, h, k, local, p, core, target):
        return pltpu.make_async_remote_copy(
            src_ref=kv_block(k, local, core, h),
            dst_ref=kv_place(h, k, p),
            send_sem=kv_send.at[kind, h, k, local],
            recv_sem=kv_recv.at[h, k, p],
            device_id=target,
            device_id_type=MESH,
        )

    def kv_local(h, k, local, p):
        return pltpu.make_async_copy(
            kv_block(k, local, s, h), kv_place(h, k, p), kv_recv.at[h, k, p]
        )

    def kv_await(h, pages):
        for k in range(2):
            for p in pages:
                pltpu.make_async_copy(
                    kv_block(0, 0, 0, 0), kv_place(h, k, p), kv_recv.at[h, k, p]
                ).wait()

    def first_local():
        return (s + jnp.where(z == TOP, sub_size, 0)) * pages_here

    def exchange(act, local_act):
        first = first_local()
        for h in range(per_core):
            for k in range(2):
                for local in range(pages_here):
                    act(kv_remote(0, h, k, local, first + local, 1 - s, {"sub": 1 - s}))
                    if local_act is not None:
                        local_act(kv_local(h, k, local, first + local))

    def hand_far(act):
        h = per_core - 1
        for k in range(2):
            for local in range(pages_here):
                act(
                    kv_remote(
                        1, h, k, local, first_local() + local, sub_size - 1,
                        {"ctx": FAR, "sub": sub_size - 1},
                    )
                )

    def hand_hub(act, held, h):
        for core in range(sub_size):
            for k in range(2):
                for local in range(held):
                    act(
                        kv_remote(
                            1 + core, h, k, local, first_local() + local, core,
                            {"ctx": HUB, "sub": core},
                        )
                    )

    def start(copy):
        copy.start()

    def sent(copy):
        copy.wait_send()

    def span_of(r):
        first, count = jnp.int32(0), jnp.int32(0)
        for i in range(REQS):
            if i < r:
                first = first + counts_ref[i]
            if i == r:
                count = counts_ref[i]
        return first * PAGE, (first + count) * PAGE - QR

    token = lax.broadcasted_iota(jnp.int32, (tok_rows, PAGE), 0)
    column = lax.broadcasted_iota(jnp.int32, (tok_rows, PAGE), 1)

    def score(task, room):
        slot, h, device, pages, (first_pos, query_base) = task
        last_seen = query_base + device * tok_rows + token
        query = jnp.concatenate(
            [qbuf[slot, h, device, :, j * HD : (j + 1) * HD] for j in range(group)], axis=0
        )
        top = jnp.full((rows, HD), NEG, jnp.float32)
        for n, p in enumerate(pages):
            keys = kvbuf[h, 0, p * PAGE : (p + 1) * PAGE, :]
            pos = p * PAGE + column
            bias = jnp.where((pos >= first_pos) & (pos <= last_seen), 0.0, NEG)
            scores = lax.dot_general(
                query, keys, (((1,), (1,)), ((), ())), preferred_element_type=jnp.float32
            )
            scores = scores.reshape(group, tok_rows, PAGE) + bias[None]
            scores = scores.reshape(rows, PAGE)
            room[:, n * PAGE : (n + 1) * PAGE] = scores
            for c in range(PAGE // HD):
                top = jnp.maximum(top, scores[:, c * HD : (c + 1) * HD])
        return top

    def weigh(task, room, top):
        slot, h, device, pages, _ = task
        top = jnp.broadcast_to(jnp.max(top, axis=1, keepdims=True), (rows, HD))
        total = jnp.zeros((rows, HD), jnp.float32)
        summed = jnp.zeros((rows, HD), jnp.float32)
        for n, p in enumerate(pages):
            parts = []
            for c in range(PAGE // HD):
                low = n * PAGE + c * HD
                parts.append(jnp.exp2((room[:, low : low + HD] - top) * factor))
                total = total + parts[-1]
            weights = jnp.concatenate([part.astype(jnp.bfloat16) for part in parts], axis=1)
            values = kvbuf[h, 1, p * PAGE : (p + 1) * PAGE, :]
            summed = summed + jnp.dot(weights, values, preferred_element_type=jnp.float32)
        done = summed / jnp.sum(total, axis=1, keepdims=True)
        done = done.astype(jnp.bfloat16)
        for j in range(group):
            obuf[slot, h, device, :, j * HD : (j + 1) * HD] = done[
                j * tok_rows : (j + 1) * tok_rows, :
            ]

    def attend(*tasks):
        rooms = (sbuf, tbuf)[: len(tasks)]
        tops = [score(task, room) for task, room in zip(tasks, rooms)]
        for task, room, top in zip(tasks, rooms, tops):
            weigh(task, room, top)

    def send_home(slot, h, device, plane, stays):
        @pl.when(stays)
        def _():
            o_local(slot, h).start()

        @pl.when(jnp.logical_not(stays))
        def _():
            o_remote(slot, h, device, plane).start()

    def turn(slot, h, i, pages, span, plane, own):
        device = lax.rem(mine - i + mates, mates)
        q_await(slot, h, device)
        attend((slot, h, device, pages, span))
        send_home(slot, h, device, plane, own & (i == 0))

    far_pages = range(split)
    near_pages = range(1, live - 2)
    hub_pages = range(2, live - 1)
    top_pages = range(split, live)
    near_or_hub = {*near_pages, *hub_pages}
    last = per_core - 1

    def stays_far(h, step):
        return (h == last) & (lax.rem(s + step, sub_size) == sub_size - 1)

    @pl.when(z == HUB)
    def _():
        hand_far(start)
        exchange(start, start)

    @pl.when((z == TOP) & (s == 0))
    def _():
        for h in range(per_core):
            hand_hub(start, pages_here, h)

    @pl.when(z == TOP)
    def _():
        exchange(start, start)

    @pl.when(z >= HUB)
    def _():
        for h in range(per_core):
            q_local(h).start()
            for step in range(1, mates):
                q_remote(h, step, z).start()

    @pl.when(z == FAR)
    def _():
        for h in range(per_core):
            for step in range(mates):
                if h < last:
                    q_remote(h, step, HUB).start()
                else:
                    keep = stays_far(h, step)

                    @pl.when(jnp.logical_not(keep))
                    def _():
                        q_remote(h, step, HUB).start()

                    @pl.when(keep)
                    def _():
                        if step:
                            q_remote(h, step, FAR).start()
                        else:
                            q_local(h).start()

        for step in range(AHEAD):
            q_remote(0, step, HUB).wait_send()
        pl.semaphore_signal(go, device_id={"ctx": NEAR}, device_id_type=MESH)

    @pl.when(z == NEAR)
    def _():
        for step in range(EARLY):
            q_remote(0, step, HUB).start()
        pl.semaphore_wait(go, 1)
        for h in range(per_core):
            for step in range(mates):
                if h or step >= EARLY:
                    q_remote(h, step, HUB).start()

    @pl.when((z == HUB) | ((z == FAR) & (s == sub_size - 1)))
    def _():
        span = span_of(FAR)
        h_low = jnp.where(z == FAR, last, 0)
        h_high = jnp.where((z == HUB) & (s == sub_size - 1), last, per_core)

        def step(n, carry):
            h, i = n // mates, n % mates

            @pl.when(i == 0)
            def _():
                kv_await(h, far_pages)

            turn(FAR, h, i, far_pages, span, FAR, z == FAR)
            return carry

        lax.fori_loop(h_low * mates, h_high * mates, step, 0)

    @pl.when(z == HUB)
    def _():
        @pl.when(s == sub_size - 1)
        def _():
            kv_await(last, far_pages)

        near_span, hub_span = span_of(NEAR), span_of(HUB)

        def both(n, carry):
            h, i = n // mates, n % mates

            @pl.when(i == 0)
            def _():
                kv_await(h, [p for p in range(live) if p >= split and p in near_or_hub])

            device = lax.rem(mine - i + mates, mates)
            q_await(NEAR, h, device)
            q_await(HUB, h, device)
            attend(
                (NEAR, h, device, near_pages, near_span), (HUB, h, device, hub_pages, hub_span)
            )
            o_remote(NEAR, h, device, NEAR).start()
            send_home(HUB, h, device, HUB, i == 0)
            return carry

        lax.fori_loop(0, per_core * mates, both, 0)

    @pl.when(z == TOP)
    def _():
        span = span_of(TOP)

        def step(n, carry):
            h, i = n // mates, n % mates

            @pl.when(i == 0)
            def _():
                kv_await(h, top_pages)

            turn(HUB, h, i, top_pages, span, TOP, True)

            @pl.when((s == 1) & (i == mates - 1))
            def _():
                hand_hub(start, 1, h)

            return carry

        lax.fori_loop(0, per_core * mates, step, 0)

    def finals():
        for h in range(per_core):
            for device in range(mates):
                pltpu.make_async_copy(
                    obuf.at[0, 0, 0], out_ref.at[:, cols(device, h)], o_recv.at[h, device]
                ).wait()

    finals()

    @pl.when(z == TOP)
    def _():
        @pl.when(s == 0)
        def _():
            for h in range(per_core):
                hand_hub(sent, pages_here, h)

        @pl.when(s == 1)
        def _():
            for h in range(per_core):
                hand_hub(sent, 1, h)

    @pl.when(z == HUB)
    def _():
        hand_far(sent)

        def drain(n, carry):
            h, device = n // mates, n % mates
            o_remote(NEAR, h, device, NEAR).wait_send()
            return carry

        lax.fori_loop(0, per_core * mates, drain, 0)

    @pl.when((z == HUB) | ((z == FAR) & (s == sub_size - 1)))
    def _():
        h_low = jnp.where(z == FAR, last, 0)
        h_high = jnp.where((z == HUB) & (s == sub_size - 1), last, per_core)

        def drain(n, carry):
            h, i = n // mates, n % mates

            @pl.when((z == HUB) | (i > 0))
            def _():
                o_remote(FAR, h, lax.rem(mine - i + mates, mates), FAR).wait_send()

            return carry

        lax.fori_loop(h_low * mates, h_high * mates, drain, 0)

    @pl.when(z >= HUB)
    def _():
        exchange(sent, None)
        for h in range(per_core):
            for step in range(1, mates):
                q_remote(h, step, z).wait_send()
                o_remote(HUB, h, lax.rem(mine + step, mates), z).wait_send()

    @pl.when(z == NEAR)
    def _():
        for h in range(per_core):
            for step in range(mates):
                q_remote(h, step, HUB).wait_send()

    @pl.when(z == FAR)
    def _():
        for h in range(last):
            for step in range(mates):
                if h or step >= AHEAD:
                    q_remote(h, step, HUB).wait_send()
        for step in range(mates):
            if step:
                q_remote(last, step, HUB).wait_send()
            else:
                @pl.when(jnp.logical_not(stays_far(last, step)))
                def _():
                    q_remote(last, step, HUB).wait_send()


def served(queries, kv_cache, page_counts):
    ctx_size, sub_size = lax.axis_size("ctx"), lax.axis_size("sub")
    head_size = lax.axis_size("head")
    pages_here = kv_cache.shape[1] // PAGE
    mates = head_size * sub_size
    per_core = KVH // mates
    group = HQ // KVH
    live = pages_here * ctx_size * sub_size // 2
    tok_rows = queries.shape[0]
    slots = ctx_size - 1
    dma = pltpu.SemaphoreType.DMA
    chunk = (slots, per_core, mates, tok_rows, group * HD)
    return pl.pallas_call(
        functools.partial(serve_kernel, (head_size, sub_size, pages_here)),
        out_shape=jax.ShapeDtypeStruct(queries.shape, jnp.bfloat16),
        in_specs=[
            pl.BlockSpec(memory_space=pltpu.SMEM),
            pl.BlockSpec(memory_space=pl.ANY),
            pl.BlockSpec(memory_space=pl.ANY),
        ],
        out_specs=pl.BlockSpec(memory_space=pl.ANY),
        scratch_shapes=[
            pltpu.VMEM((per_core, 2, live * PAGE, HD), jnp.bfloat16),
            pltpu.VMEM(chunk, jnp.bfloat16),
            pltpu.VMEM(chunk, jnp.bfloat16),
            pltpu.VMEM((group * tok_rows, (live - 3) * PAGE), jnp.float32),
            pltpu.VMEM((group * tok_rows, (live - 3) * PAGE), jnp.float32),
            dma((per_core, mates)),
            dma((slots, per_core, mates)),
            dma((slots, per_core, mates)),
            dma((per_core, mates)),
            dma((1 + sub_size, per_core, 2, pages_here)),
            dma((per_core, 2, live)),
            pltpu.SemaphoreType.REGULAR,
        ],
        compiler_params=pltpu.CompilerParams(
            collective_id=0, has_side_effects=True, vmem_limit_bytes=VMEM_LIMIT
        ),
    )(
        pltpu.with_memory_space_constraint(page_counts, pltpu.HBM),
        pltpu.with_memory_space_constraint(queries, pltpu.HBM),
        pltpu.with_memory_space_constraint(kv_cache, pltpu.HBM),
    )


def solution(mesh):
    specs = dict(
        mesh=mesh,
        in_specs=(
            P(("grp", "ctx", "head", "sub"), None),
            P(None, ("grp", "ctx", "sub"), "head"),
            P("grp"),
        ),
        out_specs=P(("grp", "ctx", "head", "sub"), None),
        check_vma=False,
    )

    def run(queries, kv_cache, page_counts):
        body = served if can_serve(mesh, kv_cache.shape[1]) else per_device
        return jax.shard_map(body, **specs)(queries, kv_cache, page_counts)

    return run
```

```python
import functools
import math

import jax
import jax.numpy as jnp
from jax import lax
from jax.experimental import pallas as pl
from jax.experimental.pallas import tpu as pltpu
from jax.sharding import PartitionSpec as P

HQ = 128
KVH = 8
HD = 128
REQS = 4
QR = 64
PAGE = 256
SPAN = 256


NEG = -1e30
MESH = pl.DeviceIdType.MESH
VMEM_LIMIT = 40000000
EARLY = 1
LATER = 4
AHEAD = 3


def from_behind(array, axis, by):
    count = lax.axis_size(axis)
    pairs = [(i, i + by) for i in range(count) if 0 <= i + by < count]
    return lax.ppermute(array, axis, pairs)


def per_device(queries, kv_cache, page_counts):
    per_group = HQ // KVH
    local_heads = kv_cache.shape[2] // HD
    ctx_size = lax.axis_size("ctx")
    sub_size = lax.axis_size("sub")
    head_count = lax.axis_size("head")
    tok_rows = queries.shape[0]
    score_scale = HD ** (-0.5)
    regrouped = lax.all_to_all(queries, "head", split_axis=1, concat_axis=0, tiled=True)
    all_queries = lax.all_gather(regrouped, ("ctx", "sub"), axis=0, tiled=True)
    all_queries = all_queries.reshape(SPAN, local_heads, per_group, HD)
    page_ends = jnp.cumsum(page_counts)
    ctx_rows = SPAN // ctx_size
    offsets = jnp.arange(QR, dtype=jnp.int32)
    columns = jnp.arange(PAGE, dtype=jnp.int32)
    flat_index = lax.axis_index("ctx") * sub_size + lax.axis_index("sub")
    pages_here = kv_cache.shape[1] // PAGE
    base_pages = pages_here * ctx_size * sub_size // 2
    initial = (
        jnp.full((SPAN, local_heads, per_group), NEG, jnp.float32),
        jnp.zeros((SPAN, local_heads, per_group), jnp.float32),
        jnp.zeros((SPAN, local_heads, per_group, HD), jnp.float32),
    )
    half_rows = kv_cache.shape[1] // 2
    arrived = from_behind(kv_cache[:, half_rows:], "ctx", -(ctx_size // 2))
    is_lower = lax.axis_index("ctx") < ctx_size // 2
    source_flat = flat_index + ctx_size // 2 * sub_size
    working = jnp.where(is_lower, arrived, kv_cache[:, :half_rows])
    first_page = jnp.where(
        is_lower, source_flat * pages_here + pages_here // 2, flat_index * pages_here
    )
    page_total = working.shape[1] // PAGE

    def add_page(page_turn, running):
        page_index = first_page + page_turn
        relative = page_index - base_pages
        counted = jnp.sum((relative >= page_ends).astype(jnp.int32))
        request = jnp.where(relative < 0, REQS, counted)

        def update(partial_value):
            run_max, run_sum, run_out = partial_value
            request_id = jnp.minimum(request, REQS - 1)
            row_start = request_id * QR
            gathered = row_start + offsets
            within = gathered % ctx_rows
            ctx_block = gathered // ctx_rows
            sub_part = within // (head_count * tok_rows)
            head_part = within // tok_rows % head_count
            tok_part = within % tok_rows
            natural = ctx_block * ctx_rows + (head_part * sub_size + sub_part) * tok_rows + tok_part
            query_pos = (page_ends[request_id] + base_pages) * PAGE - QR + natural - row_start
            key_pos = page_index * PAGE + columns
            visible = key_pos[None, :] <= query_pos[:, None]
            page_keys = working[0].reshape(PAGE, local_heads, HD)
            page_values = working[1].reshape(PAGE, local_heads, HD)
            query_rows = lax.dynamic_slice_in_dim(all_queries, row_start, QR, 0)
            scores = (
                jnp.einsum(
                    "qkgd,pkd->qkgp", query_rows, page_keys, preferred_element_type=jnp.float32
                )
                * score_scale
            )
            scores = jnp.where(visible[:, None, None, :], scores, NEG)
            old_max = lax.dynamic_slice_in_dim(run_max, row_start, QR, 0)
            old_sum = lax.dynamic_slice_in_dim(run_sum, row_start, QR, 0)
            old_out = lax.dynamic_slice_in_dim(run_out, row_start, QR, 0)
            new_max = jnp.maximum(old_max, jnp.max(scores, axis=3))
            factor = jnp.exp(old_max - new_max)
            numerators = jnp.exp(scores - new_max[..., None])
            new_sum = old_sum * factor + jnp.sum(numerators, axis=3)
            product = jnp.einsum(
                "qkgp,pkd->qkgd",
                numerators.astype(jnp.bfloat16),
                page_values,
                preferred_element_type=jnp.float32,
            )
            new_out = old_out * factor[..., None] + product
            return (
                lax.dynamic_update_slice_in_dim(run_max, new_max, row_start, 0),
                lax.dynamic_update_slice_in_dim(run_sum, new_sum, row_start, 0),
                lax.dynamic_update_slice_in_dim(run_out, new_out, row_start, 0),
            )

        def unchanged(partial_value):
            return partial_value

        return lax.cond(request < REQS, update, unchanged, running)

    run_max, run_sum, run_out = lax.fori_loop(0, page_total, add_page, initial)
    share = SPAN // (ctx_size * sub_size)
    global_max = lax.pmax(run_max, ("ctx", "sub"))
    factor = jnp.exp(run_max - global_max)
    sums_here, outs_here = (
        lax.psum_scatter(
            (run_sum * factor).astype(jnp.bfloat16), ("ctx", "sub"), scatter_dimension=0, tiled=True
        ).astype(jnp.float32),
        lax.psum_scatter(
            (run_out * factor[..., None]).astype(jnp.bfloat16),
            ("ctx", "sub"),
            scatter_dimension=0,
            tiled=True,
        ).astype(jnp.float32),
    )
    finished = (outs_here / sums_here[..., None]).astype(jnp.bfloat16)
    finished = finished.reshape(share, local_heads * per_group * HD)
    return lax.all_to_all(finished, "head", split_axis=0, concat_axis=1, tiled=True)


FAR, NEAR, HUB, TOP = range(4)


def can_serve(mesh, rows):
    ctx_size, sub_size, head_size = mesh.shape["ctx"], mesh.shape["sub"], mesh.shape["head"]
    if ctx_size != REQS or SPAN // ctx_size != QR or sub_size != 2:
        return False
    pages_here = rows // (mesh.shape["grp"] * ctx_size * sub_size) // PAGE
    return pages_here == 2 and head_size == 2 and KVH == 2 * head_size * sub_size


def serve_kernel(
    sizes,
    counts_hbm,
    q_hbm,
    kv_hbm,
    out_ref,
    counts_ref,
    kvbuf,
    qbuf,
    obuf,
    sbuf,
    tbuf,
    counts_sem,
    q_send,
    q_recv,
    own_recv,
    o_send,
    o_recv,
    kv_send,
    kv_recv,
    go,
):
    head_size, sub_size, pages_here = sizes
    mates = head_size * sub_size
    per_core = KVH // mates
    group = HQ // KVH
    width = group * HD
    tok_rows = QR // mates
    rows = group * tok_rows
    split = pages_here * sub_size
    live = 2 * split
    z, x, s = lax.axis_index("ctx"), lax.axis_index("head"), lax.axis_index("sub")
    mine = x * sub_size + s
    slot_of = jnp.minimum(z, HUB)
    factor = HD ** (-0.5) * math.log2(math.e)

    def at(device, plane=None):
        place = {"head": device // sub_size, "sub": device % sub_size}
        if plane is not None:
            place["ctx"] = plane
        return place

    barrier = pltpu.get_barrier_semaphore()
    counts_copy = pltpu.make_async_copy(counts_hbm, counts_ref, counts_sem.at[0])
    counts_copy.start()

    def greet(place):
        pl.semaphore_signal(barrier, device_id=place, device_id_type=MESH)

    def greet_plane(plane):
        for device in range(mates):
            greet(at(device, plane))

    def greet_mates():
        for step in range(1, mates):
            greet(at(lax.rem(mine + step, mates)))

    @pl.when(z == HUB)
    def _():
        greet_mates()
        greet_plane(FAR)
        greet_plane(NEAR)
        for core in range(sub_size):
            greet({"ctx": TOP, "sub": core})
        pl.semaphore_wait(barrier, 3 * mates - 1)

    @pl.when(z == TOP)
    def _():
        greet_mates()
        pl.semaphore_wait(barrier, mates - 1 + sub_size)

    @pl.when(z == NEAR)
    def _():
        greet_plane(HUB)
        greet({"ctx": FAR})
        pl.semaphore_wait(barrier, mates)

    @pl.when(z == FAR)
    def _():
        greet_plane(HUB)
        greet_mates()
        pl.semaphore_wait(barrier, 2 * mates)

    counts_copy.wait()

    def partner(h, step):
        turned = jnp.where(h == 0, step, mates - 1 - step)
        far_x, far_s = turned // sub_size, turned % sub_size
        return lax.rem(x + far_x, head_size) * sub_size + lax.rem(s + far_s, sub_size)

    def alone(h, step):
        return jnp.where(h == 0, step, mates - 1 - step) == 0

    def cols(device, h):
        return pl.ds(pl.multiple_of((device * per_core + h) * width, width), width)

    def q_remote(h, step, plane, recv, part=1):
        other = partner(h, step)
        return pltpu.make_async_remote_copy(
            src_ref=q_hbm.at[:, cols(other, h)],
            dst_ref=qbuf.at[slot_of, h, mine],
            send_sem=q_send.at[part],
            recv_sem=recv,
            device_id=at(other, plane),
            device_id_type=MESH,
        )

    def q_local(h, recv):
        return pltpu.make_async_copy(q_hbm.at[:, cols(mine, h)], qbuf.at[slot_of, h, mine], recv)

    def q_await(slot, h, device):
        pltpu.make_async_copy(
            q_hbm.at[:, cols(0, 0)], qbuf.at[slot, h, device], q_recv.at[slot, h, device]
        ).wait()

    def own_await(h):
        pltpu.make_async_copy(obuf.at[HUB, h], qbuf.at[HUB, h], own_recv.at[h]).wait()

    def o_remote(slot, h, device, plane):
        return pltpu.make_async_remote_copy(
            src_ref=obuf.at[slot, h, device],
            dst_ref=out_ref.at[:, cols(mine, h)],
            send_sem=o_send.at[slot],
            recv_sem=o_recv.at[0],
            device_id=at(device, plane),
            device_id_type=MESH,
        )

    def o_local(slot, h):
        return pltpu.make_async_copy(
            obuf.at[slot, h, mine], out_ref.at[:, cols(mine, h)], o_recv.at[0]
        )

    def settle(sem, chunks):
        span = pl.ds(0, chunks * width)
        pltpu.make_async_copy(q_hbm.at[:, span], out_ref.at[:, span], sem).wait()

    def settle_kv(blocks):
        span = pl.ds(0, blocks * PAGE // (2 * per_core))
        pltpu.make_async_copy(kvbuf.at[:, :, span], kvbuf.at[:, :, span], kv_send.at[0]).wait()

    def kv_block(core, h, held):
        return kv_hbm.at[
            :,
            pl.ds(0, held * PAGE),
            pl.ds(pl.multiple_of((core * per_core + h) * HD, HD), HD),
        ]

    def kv_place(h, p, held):
        return kvbuf.at[h, :, pl.ds(pl.multiple_of(p * PAGE, PAGE), held * PAGE)]

    here = (s + jnp.where(z == TOP, sub_size, 0)) * pages_here
    half = jnp.where(z == TOP, 1, 0)

    def kv_remote(h, core, held, target):
        return pltpu.make_async_remote_copy(
            src_ref=kv_block(core, h, held),
            dst_ref=kv_place(h, here, held),
            send_sem=kv_send.at[0],
            recv_sem=kv_recv.at[h, half],
            device_id=target,
            device_id_type=MESH,
        )

    def kv_await(h, first, count):
        place = kv_place(h, first, count)
        pltpu.make_async_copy(place, place, kv_recv.at[h, 0 if first < split else 1]).wait()

    def exchange():
        for h in range(per_core):
            kv_remote(h, 1 - s, pages_here, {"sub": 1 - s}).start()
            pltpu.make_async_copy(
                kv_block(s, h, pages_here), kv_place(h, here, pages_here), kv_recv.at[h, half]
            ).start()

    def hand_far():
        core = sub_size - 1
        kv_remote(per_core - 1, core, pages_here, {"ctx": FAR, "sub": core}).start()

    def hand_hub(held, h):
        for core in reversed(range(sub_size)):
            kv_remote(h, core, held, {"ctx": HUB, "sub": core}).start()

    def span_of(r):
        first, count = jnp.int32(0), jnp.int32(0)
        for i in range(REQS):
            if i < r:
                first = first + counts_ref[i]
            if i == r:
                count = counts_ref[i]
        return first * PAGE, (first + count) * PAGE - QR

    token = lax.broadcasted_iota(jnp.int32, (tok_rows, PAGE), 0)
    column = lax.broadcasted_iota(jnp.int32, (tok_rows, PAGE), 1)

    def score(task, room):
        slot, h, device, pages, (first_pos, query_base) = task
        last_seen = query_base + device * tok_rows + token
        query = jnp.concatenate(
            [qbuf[slot, h, device, :, j * HD : (j + 1) * HD] for j in range(group)], axis=0
        )
        top = jnp.full((rows, HD), NEG, jnp.float32)
        for n, p in enumerate(pages):
            keys = kvbuf[h, 0, p * PAGE : (p + 1) * PAGE, :]
            pos = p * PAGE + column
            bias = jnp.where((pos >= first_pos) & (pos <= last_seen), 0.0, NEG)
            scores = lax.dot_general(
                query, keys, (((1,), (1,)), ((), ())), preferred_element_type=jnp.float32
            )
            scores = scores.reshape(group, tok_rows, PAGE) + bias[None]
            scores = scores.reshape(rows, PAGE)
            room[:, n * PAGE : (n + 1) * PAGE] = scores
            for c in range(PAGE // HD):
                top = jnp.maximum(top, scores[:, c * HD : (c + 1) * HD])
        return top

    def weigh(task, room, top):
        slot, h, device, pages, _ = task
        top = jnp.broadcast_to(jnp.max(top, axis=1, keepdims=True), (rows, HD))
        total = jnp.zeros((rows, HD), jnp.float32)
        summed = jnp.zeros((rows, HD), jnp.float32)
        for n, p in enumerate(pages):
            parts = []
            for c in range(PAGE // HD):
                low = n * PAGE + c * HD
                parts.append(jnp.exp2((room[:, low : low + HD] - top) * factor))
                total = total + parts[-1]
            weights = jnp.concatenate([part.astype(jnp.bfloat16) for part in parts], axis=1)
            values = kvbuf[h, 1, p * PAGE : (p + 1) * PAGE, :]
            summed = summed + jnp.dot(weights, values, preferred_element_type=jnp.float32)
        done = summed / jnp.sum(total, axis=1, keepdims=True)
        done = done.astype(jnp.bfloat16)
        for j in range(group):
            obuf[slot, h, device, :, j * HD : (j + 1) * HD] = done[
                j * tok_rows : (j + 1) * tok_rows, :
            ]

    def attend(*tasks):
        rooms = (sbuf, tbuf)[: len(tasks)]
        tops = [score(task, room) for task, room in zip(tasks, rooms)]
        for task, room, top in zip(tasks, rooms, tops):
            weigh(task, room, top)

    def send_home(slot, h, device, plane, stays):
        @pl.when(stays)
        def _():
            o_local(slot, h).start()

        @pl.when(jnp.logical_not(stays))
        def _():
            o_remote(slot, h, device, plane).start()

    def turn(slot, h, i, pages, span, plane, own):
        device = partner(h, i)
        attend((slot, h, device, pages, span))
        send_home(slot, h, device, plane, own & alone(h, i))

    far_pages = range(split)
    near_pages = range(1, live - 2)
    hub_pages = range(2, live - 1)
    top_pages = range(split, live)
    last = per_core - 1

    def stays_far(step):
        return lax.rem(partner(last, step), sub_size) == sub_size - 1

    @pl.when(z == HUB)
    def _():
        hand_far()
        exchange()

    @pl.when((z == TOP) & (s == 0))
    def _():
        for h in range(per_core):
            hand_hub(pages_here, h)

    @pl.when((z == TOP) & (s == 1))
    def _():
        hand_hub(1, 0)

    @pl.when(z == TOP)
    def _():
        exchange()

    @pl.when(z >= HUB)
    def _():
        for h in range(per_core):
            q_local(h, own_recv.at[h]).start()
            for step in range(mates):
                if (step, mates - 1 - step)[h != 0]:
                    q_remote(h, step, z, own_recv.at[h]).start()

    @pl.when(z == FAR)
    def _():
        for h in range(per_core):
            recv = q_recv.at[FAR, h, mine]
            for step in range(mates):
                if h < last:
                    q_remote(h, step, HUB, recv, 0 if step < AHEAD else 1).start()
                else:
                    keep = stays_far(step)

                    @pl.when(jnp.logical_not(keep))
                    def _():
                        q_remote(h, step, HUB, recv).start()

                    @pl.when(keep)
                    def _():
                        if mates - 1 - step:
                            q_remote(h, step, FAR, recv).start()
                        else:
                            q_local(h, recv).start()

        settle(q_send.at[0], AHEAD)
        pl.semaphore_signal(go, device_id={"ctx": NEAR}, device_id_type=MESH)

    @pl.when(z == NEAR)
    def _():
        for step in range(EARLY):
            q_remote(0, step, HUB, q_recv.at[NEAR, 0, mine]).start()
        pl.semaphore_wait(go, 1)
        for h in range(per_core):
            for step in range(mates):
                if h or step >= EARLY:
                    q_remote(h, step, HUB, q_recv.at[NEAR, h, mine]).start()

    @pl.when((z == HUB) | ((z == FAR) & (s == sub_size - 1)))
    def _():
        span = span_of(FAR)
        h_low = jnp.where(z == FAR, last, 0)
        h_high = jnp.where((z == HUB) & (s == sub_size - 1), last, per_core)

        def step(n, carry):
            h, i = n // mates, n % mates

            @pl.when(i == 0)
            def _():
                kv_await(h, 0, split)

            q_await(FAR, h, partner(h, i))
            turn(FAR, h, i, far_pages, span, FAR, z == FAR)
            return carry

        lax.fori_loop(h_low * mates, h_high * mates, step, 0)

    @pl.when(z == HUB)
    def _():
        @pl.when(s == sub_size - 1)
        def _():
            kv_await(last, 0, split)

        near_span, hub_span = span_of(NEAR), span_of(HUB)

        def both(n, carry):
            h, i = n // mates, n % mates

            @pl.when(i == 0)
            def _():
                own_await(h)
                kv_await(h, split, split - 1)

            device = partner(h, i)
            q_await(NEAR, h, device)
            attend(
                (NEAR, h, device, near_pages, near_span), (HUB, h, device, hub_pages, hub_span)
            )
            o_remote(NEAR, h, device, NEAR).start()
            send_home(HUB, h, device, HUB, alone(h, i))
            return carry

        lax.fori_loop(0, per_core * mates, both, 0)

    @pl.when(z == TOP)
    def _():
        span = span_of(TOP)

        def step(n, carry):
            h, i = n // mates, n % mates

            @pl.when(i == 0)
            def _():
                own_await(h)
                kv_await(h, split, split)

            turn(HUB, h, i, top_pages, span, TOP, True)

            @pl.when((s == 1) & (n == LATER))
            def _():
                hand_hub(1, last)

            return carry

        lax.fori_loop(0, per_core * mates, step, 0)

    def finals():
        settle(o_recv.at[0], per_core * mates)

    finals()

    @pl.when(z == HUB)
    def _():
        settle_kv(2 * pages_here * (per_core + 1))
        settle(o_send.at[NEAR], per_core * mates)

        @pl.when(s == 0)
        def _():
            settle(o_send.at[FAR], per_core * mates)

        @pl.when(s == 1)
        def _():
            settle(o_send.at[FAR], last * mates)

    @pl.when(z == TOP)
    def _():
        @pl.when(s == 0)
        def _():
            settle_kv(2 * pages_here * per_core * (1 + sub_size))

        @pl.when(s == 1)
        def _():
            settle_kv(2 * per_core * (pages_here + sub_size))

    @pl.when(z >= HUB)
    def _():
        settle(q_send.at[1], per_core * (mates - 1))
        settle(o_send.at[HUB], per_core * (mates - 1))

    @pl.when(z == NEAR)
    def _():
        settle(q_send.at[1], per_core * mates)

    @pl.when((z == FAR) & (s == 0))
    def _():
        settle(q_send.at[1], per_core * mates - AHEAD)

    @pl.when((z == FAR) & (s == 1))
    def _():
        settle(q_send.at[1], per_core * mates - 1 - AHEAD)
        settle(o_send.at[FAR], mates - 1)


def served(queries, kv_cache, page_counts):
    ctx_size, sub_size = lax.axis_size("ctx"), lax.axis_size("sub")
    head_size = lax.axis_size("head")
    pages_here = kv_cache.shape[1] // PAGE
    mates = head_size * sub_size
    per_core = KVH // mates
    group = HQ // KVH
    live = pages_here * ctx_size * sub_size // 2
    tok_rows = queries.shape[0]
    slots = ctx_size - 1
    dma = pltpu.SemaphoreType.DMA
    chunk = (slots, per_core, mates, tok_rows, group * HD)
    return pl.pallas_call(
        functools.partial(serve_kernel, (head_size, sub_size, pages_here)),
        out_shape=jax.ShapeDtypeStruct(queries.shape, jnp.bfloat16),
        in_specs=[
            pl.BlockSpec(memory_space=pl.ANY),
            pl.BlockSpec(memory_space=pl.ANY),
            pl.BlockSpec(memory_space=pl.ANY),
        ],
        out_specs=pl.BlockSpec(memory_space=pl.ANY),
        scratch_shapes=[
            pltpu.SMEM((REQS,), jnp.int32),
            pltpu.VMEM((per_core, 2, live * PAGE, HD), jnp.bfloat16),
            pltpu.VMEM(chunk, jnp.bfloat16),
            pltpu.VMEM(chunk, jnp.bfloat16),
            pltpu.VMEM((group * tok_rows, (live - 3) * PAGE), jnp.float32),
            pltpu.VMEM((group * tok_rows, (live - 3) * PAGE), jnp.float32),
            dma((1,)),
            dma((2,)),
            dma((slots - 1, per_core, mates)),
            dma((per_core,)),
            dma((slots,)),
            dma((1,)),
            dma((1,)),
            dma((per_core, 2)),
            pltpu.SemaphoreType.REGULAR,
        ],
        compiler_params=pltpu.CompilerParams(
            collective_id=0, has_side_effects=True, vmem_limit_bytes=VMEM_LIMIT
        ),
    )(
        pltpu.with_memory_space_constraint(page_counts, pltpu.HBM),
        pltpu.with_memory_space_constraint(queries, pltpu.HBM),
        pltpu.with_memory_space_constraint(kv_cache, pltpu.HBM),
    )


def solution(mesh):
    specs = dict(
        mesh=mesh,
        in_specs=(
            P(("grp", "ctx", "head", "sub"), None),
            P(None, ("grp", "ctx", "sub"), "head"),
            P("grp"),
        ),
        out_specs=P(("grp", "ctx", "head", "sub"), None),
        check_vma=False,
    )

    def run(queries, kv_cache, page_counts):
        body = served if can_serve(mesh, kv_cache.shape[1]) else per_device
        return jax.shard_map(body, **specs)(queries, kv_cache, page_counts)

    return run
```

```python
import functools
import math

import jax
import jax.numpy as jnp
from jax import lax
from jax.experimental import pallas as pl
from jax.experimental.pallas import tpu as pltpu
from jax.sharding import PartitionSpec as P

HQ = 128
KVH = 8
HD = 128
REQS = 4
QR = 64
PAGE = 256
SPAN = 256


NEG = -1e30
MESH = pl.DeviceIdType.MESH
VMEM_LIMIT = 40000000
EARLY = 1
WHEN = 2
OWN = 2
LAG = 2
AHEAD = 3


def from_behind(array, axis, by):
    count = lax.axis_size(axis)
    pairs = [(i, i + by) for i in range(count) if 0 <= i + by < count]
    return lax.ppermute(array, axis, pairs)


def per_device(queries, kv_cache, page_counts):
    per_group = HQ // KVH
    local_heads = kv_cache.shape[2] // HD
    ctx_size = lax.axis_size("ctx")
    sub_size = lax.axis_size("sub")
    head_count = lax.axis_size("head")
    tok_rows = queries.shape[0]
    score_scale = HD ** (-0.5)
    regrouped = lax.all_to_all(queries, "head", split_axis=1, concat_axis=0, tiled=True)
    all_queries = lax.all_gather(regrouped, ("ctx", "sub"), axis=0, tiled=True)
    all_queries = all_queries.reshape(SPAN, local_heads, per_group, HD)
    page_ends = jnp.cumsum(page_counts)
    ctx_rows = SPAN // ctx_size
    offsets = jnp.arange(QR, dtype=jnp.int32)
    columns = jnp.arange(PAGE, dtype=jnp.int32)
    flat_index = lax.axis_index("ctx") * sub_size + lax.axis_index("sub")
    pages_here = kv_cache.shape[1] // PAGE
    base_pages = pages_here * ctx_size * sub_size // 2
    initial = (
        jnp.full((SPAN, local_heads, per_group), NEG, jnp.float32),
        jnp.zeros((SPAN, local_heads, per_group), jnp.float32),
        jnp.zeros((SPAN, local_heads, per_group, HD), jnp.float32),
    )
    half_rows = kv_cache.shape[1] // 2
    arrived = from_behind(kv_cache[:, half_rows:], "ctx", -(ctx_size // 2))
    is_lower = lax.axis_index("ctx") < ctx_size // 2
    source_flat = flat_index + ctx_size // 2 * sub_size
    working = jnp.where(is_lower, arrived, kv_cache[:, :half_rows])
    first_page = jnp.where(
        is_lower, source_flat * pages_here + pages_here // 2, flat_index * pages_here
    )
    page_total = working.shape[1] // PAGE

    def add_page(page_turn, running):
        page_index = first_page + page_turn
        relative = page_index - base_pages
        counted = jnp.sum((relative >= page_ends).astype(jnp.int32))
        request = jnp.where(relative < 0, REQS, counted)

        def update(partial_value):
            run_max, run_sum, run_out = partial_value
            request_id = jnp.minimum(request, REQS - 1)
            row_start = request_id * QR
            gathered = row_start + offsets
            within = gathered % ctx_rows
            ctx_block = gathered // ctx_rows
            sub_part = within // (head_count * tok_rows)
            head_part = within // tok_rows % head_count
            tok_part = within % tok_rows
            natural = ctx_block * ctx_rows + (head_part * sub_size + sub_part) * tok_rows + tok_part
            query_pos = (page_ends[request_id] + base_pages) * PAGE - QR + natural - row_start
            key_pos = page_index * PAGE + columns
            visible = key_pos[None, :] <= query_pos[:, None]
            page_keys = working[0].reshape(PAGE, local_heads, HD)
            page_values = working[1].reshape(PAGE, local_heads, HD)
            query_rows = lax.dynamic_slice_in_dim(all_queries, row_start, QR, 0)
            scores = (
                jnp.einsum(
                    "qkgd,pkd->qkgp", query_rows, page_keys, preferred_element_type=jnp.float32
                )
                * score_scale
            )
            scores = jnp.where(visible[:, None, None, :], scores, NEG)
            old_max = lax.dynamic_slice_in_dim(run_max, row_start, QR, 0)
            old_sum = lax.dynamic_slice_in_dim(run_sum, row_start, QR, 0)
            old_out = lax.dynamic_slice_in_dim(run_out, row_start, QR, 0)
            new_max = jnp.maximum(old_max, jnp.max(scores, axis=3))
            factor = jnp.exp(old_max - new_max)
            numerators = jnp.exp(scores - new_max[..., None])
            new_sum = old_sum * factor + jnp.sum(numerators, axis=3)
            product = jnp.einsum(
                "qkgp,pkd->qkgd",
                numerators.astype(jnp.bfloat16),
                page_values,
                preferred_element_type=jnp.float32,
            )
            new_out = old_out * factor[..., None] + product
            return (
                lax.dynamic_update_slice_in_dim(run_max, new_max, row_start, 0),
                lax.dynamic_update_slice_in_dim(run_sum, new_sum, row_start, 0),
                lax.dynamic_update_slice_in_dim(run_out, new_out, row_start, 0),
            )

        def unchanged(partial_value):
            return partial_value

        return lax.cond(request < REQS, update, unchanged, running)

    run_max, run_sum, run_out = lax.fori_loop(0, page_total, add_page, initial)
    share = SPAN // (ctx_size * sub_size)
    global_max = lax.pmax(run_max, ("ctx", "sub"))
    factor = jnp.exp(run_max - global_max)
    sums_here, outs_here = (
        lax.psum_scatter(
            (run_sum * factor).astype(jnp.bfloat16), ("ctx", "sub"), scatter_dimension=0, tiled=True
        ).astype(jnp.float32),
        lax.psum_scatter(
            (run_out * factor[..., None]).astype(jnp.bfloat16),
            ("ctx", "sub"),
            scatter_dimension=0,
            tiled=True,
        ).astype(jnp.float32),
    )
    finished = (outs_here / sums_here[..., None]).astype(jnp.bfloat16)
    finished = finished.reshape(share, local_heads * per_group * HD)
    return lax.all_to_all(finished, "head", split_axis=0, concat_axis=1, tiled=True)


FAR, NEAR, HUB, TOP = range(4)


def can_serve(mesh, rows):
    ctx_size, sub_size, head_size = mesh.shape["ctx"], mesh.shape["sub"], mesh.shape["head"]
    if ctx_size != REQS or SPAN // ctx_size != QR or sub_size != 2:
        return False
    pages_here = rows // (mesh.shape["grp"] * ctx_size * sub_size) // PAGE
    return pages_here == 2 and head_size == 2 and KVH == 2 * head_size * sub_size


def serve_kernel(
    sizes,
    counts_hbm,
    q_hbm,
    kv_hbm,
    out_ref,
    counts_ref,
    kvbuf,
    qbuf,
    obuf,
    sbuf,
    tbuf,
    counts_sem,
    q_send,
    q_recv,
    own_recv,
    o_send,
    o_recv,
    kv_send,
    kv_recv,
    go,
):
    head_size, sub_size, pages_here = sizes
    mates = head_size * sub_size
    per_core = KVH // mates
    group = HQ // KVH
    width = group * HD
    tok_rows = QR // mates
    rows = group * tok_rows
    split = pages_here * sub_size
    live = 2 * split
    z, x, s = lax.axis_index("ctx"), lax.axis_index("head"), lax.axis_index("sub")
    mine = x * sub_size + s
    slot_of = jnp.minimum(z, HUB)
    factor = HD ** (-0.5) * math.log2(math.e)

    def at(device, plane=None):
        place = {"head": device // sub_size, "sub": device % sub_size}
        if plane is not None:
            place["ctx"] = plane
        return place

    barrier = pltpu.get_barrier_semaphore()
    counts_copy = pltpu.make_async_copy(counts_hbm, counts_ref, counts_sem.at[0])
    counts_copy.start()

    def greet(place):
        pl.semaphore_signal(barrier, device_id=place, device_id_type=MESH)

    def greet_plane(plane):
        for device in range(mates):
            greet(at(device, plane))

    def greet_column(plane):
        for core in range(sub_size):
            greet({"ctx": plane, "sub": core})

    def greet_mates():
        for step in range(1, mates):
            greet(at(lax.rem(mine + step, mates)))

    def vouch(plane):
        pl.semaphore_signal(go, device_id={"ctx": plane}, device_id_type=MESH)

    @pl.when(z == HUB)
    def _():
        greet_column(NEAR)
        greet_column(FAR)
        greet_plane(TOP)
        pl.semaphore_wait(barrier, sub_size)

    @pl.when(z == TOP)
    def _():
        greet_mates()
        pl.semaphore_wait(barrier, 4 * mates - 1)
        vouch(HUB)
        vouch(FAR)
        vouch(NEAR)

    @pl.when(z == NEAR)
    def _():
        greet_plane(TOP)
        pl.semaphore_wait(barrier, sub_size)

    @pl.when(z == FAR)
    def _():
        greet_column(HUB)
        greet_plane(TOP)
        pl.semaphore_wait(barrier, sub_size)

    def partner(h, step):
        turned = jnp.where(h == 0, step, mates - 1 - step)
        far_x, far_s = turned // sub_size, turned % sub_size
        return lax.rem(x + far_x, head_size) * sub_size + lax.rem(s + far_s, sub_size)

    def alone(h, step):
        return jnp.where(h == 0, step, mates - 1 - step) == 0

    def cols(device, h):
        return pl.ds(pl.multiple_of((device * per_core + h) * width, width), width)

    def q_remote(h, step, plane, recv, part=1):
        other = partner(h, step)
        return pltpu.make_async_remote_copy(
            src_ref=q_hbm.at[:, cols(other, h)],
            dst_ref=qbuf.at[slot_of, h, mine],
            send_sem=q_send.at[part],
            recv_sem=recv,
            device_id=at(other, plane),
            device_id_type=MESH,
        )

    def q_local(h, recv):
        return pltpu.make_async_copy(q_hbm.at[:, cols(mine, h)], qbuf.at[slot_of, h, mine], recv)

    def q_await(slot, h, device):
        pltpu.make_async_copy(
            q_hbm.at[:, cols(0, 0)], qbuf.at[slot, h, device], q_recv.at[slot, h, device]
        ).wait()

    def own_await(h):
        pltpu.make_async_copy(obuf.at[HUB, h], qbuf.at[HUB, h], own_recv.at[h]).wait()

    def o_remote(slot, h, device, plane):
        return pltpu.make_async_remote_copy(
            src_ref=obuf.at[slot, h, device],
            dst_ref=out_ref.at[:, cols(mine, h)],
            send_sem=o_send.at[slot],
            recv_sem=o_recv.at[0],
            device_id=at(device, plane),
            device_id_type=MESH,
        )

    def o_local(slot, h):
        return pltpu.make_async_copy(
            obuf.at[slot, h, mine], out_ref.at[:, cols(mine, h)], o_recv.at[0]
        )

    def settle(sem, chunks):
        span = pl.ds(0, chunks * width)
        pltpu.make_async_copy(q_hbm.at[:, span], out_ref.at[:, span], sem).wait()

    def settle_kv(blocks, part=0):
        span = pl.ds(0, blocks * PAGE // (2 * per_core))
        pltpu.make_async_copy(kvbuf.at[:, :, span], kvbuf.at[:, :, span], kv_send.at[part]).wait()

    def kv_block(core, h, held, skip=0):
        return kv_hbm.at[
            :,
            pl.ds(skip * PAGE, held * PAGE),
            pl.ds(pl.multiple_of((core * per_core + h) * HD, HD), HD),
        ]

    def kv_place(h, p, held):
        return kvbuf.at[h, :, pl.ds(pl.multiple_of(p * PAGE, PAGE), held * PAGE)]

    here = (s + jnp.where(z == TOP, sub_size, 0)) * pages_here
    half = jnp.where(z == TOP, 1, 0)

    def kv_remote(h, core, held, target, recv, part=0, skip=0):
        return pltpu.make_async_remote_copy(
            src_ref=kv_block(core, h, held, skip),
            dst_ref=kv_place(h, here + skip, held),
            send_sem=kv_send.at[part],
            recv_sem=kv_recv.at[h, recv],
            device_id=target,
            device_id_type=MESH,
        )

    def kv_await(h, first, count):
        place = kv_place(h, first, count)
        recv = 0 if first < split else (1 if first == split else 2)
        pltpu.make_async_copy(place, place, kv_recv.at[h, recv]).wait()

    def own_pages():
        for h in range(per_core):
            pltpu.make_async_copy(
                kv_block(s, h, pages_here), kv_place(h, here, pages_here), kv_recv.at[h, half]
            ).start()

    def exchange():
        for h in range(per_core):
            kv_remote(h, 1 - s, pages_here, {"sub": 1 - s}, half).start()

    def hand_far():
        core = sub_size - 1
        kv_remote(
            per_core - 1, core, pages_here, {"ctx": FAR, "sub": core}, 0
        ).start()

    last = per_core - 1

    def hand_hub(held, h, recv):
        for core in reversed(range(sub_size)):
            target = {"ctx": HUB, "sub": core}
            if core == 0 and h == last and held > 1:
                kv_remote(h, core, held - 1, target, recv, 1).start()
                kv_remote(h, core, 1, target, recv, 2, held - 1).start()
            else:
                kv_remote(h, core, held, target, recv, 1).start()

    def span_of(r):
        first, count = jnp.int32(0), jnp.int32(0)
        for i in range(REQS):
            if i < r:
                first = first + counts_ref[i]
            if i == r:
                count = counts_ref[i]
        return first * PAGE, (first + count) * PAGE - QR

    token = lax.broadcasted_iota(jnp.int32, (tok_rows, PAGE), 0)
    column = lax.broadcasted_iota(jnp.int32, (tok_rows, PAGE), 1)

    def score(task, room):
        slot, h, device, pages, (first_pos, query_base) = task
        last_seen = query_base + device * tok_rows + token
        query = jnp.concatenate(
            [qbuf[slot, h, device, :, j * HD : (j + 1) * HD] for j in range(group)], axis=0
        )
        top = jnp.full((rows, HD), NEG, jnp.float32)
        for n, p in enumerate(pages):
            keys = kvbuf[h, 0, p * PAGE : (p + 1) * PAGE, :]
            pos = p * PAGE + column
            bias = jnp.where((pos >= first_pos) & (pos <= last_seen), 0.0, NEG)
            scores = lax.dot_general(
                query, keys, (((1,), (1,)), ((), ())), preferred_element_type=jnp.float32
            )
            scores = scores.reshape(group, tok_rows, PAGE) + bias[None]
            scores = scores.reshape(rows, PAGE)
            room[:, n * PAGE : (n + 1) * PAGE] = scores
            for c in range(PAGE // HD):
                top = jnp.maximum(top, scores[:, c * HD : (c + 1) * HD])
        return top

    def weigh(task, room, top):
        slot, h, device, pages, _ = task
        top = jnp.broadcast_to(jnp.max(top, axis=1, keepdims=True), (rows, HD))
        total = jnp.zeros((rows, HD), jnp.float32)
        summed = jnp.zeros((rows, HD), jnp.float32)
        for n, p in enumerate(pages):
            parts = []
            for c in range(PAGE // HD):
                low = n * PAGE + c * HD
                parts.append(jnp.exp2((room[:, low : low + HD] - top) * factor))
                total = total + parts[-1]
            weights = jnp.concatenate([part.astype(jnp.bfloat16) for part in parts], axis=1)
            values = kvbuf[h, 1, p * PAGE : (p + 1) * PAGE, :]
            summed = summed + jnp.dot(weights, values, preferred_element_type=jnp.float32)
        done = summed / jnp.sum(total, axis=1, keepdims=True)
        done = done.astype(jnp.bfloat16)
        for j in range(group):
            obuf[slot, h, device, :, j * HD : (j + 1) * HD] = done[
                j * tok_rows : (j + 1) * tok_rows, :
            ]

    def attend(*tasks):
        rooms = (sbuf, tbuf)[: len(tasks)]
        tops = [score(task, room) for task, room in zip(tasks, rooms)]
        for task, room, top in zip(tasks, rooms, tops):
            weigh(task, room, top)

    def send_home(slot, h, device, plane, stays):
        @pl.when(stays)
        def _():
            o_local(slot, h).start()

        @pl.when(jnp.logical_not(stays))
        def _():
            o_remote(slot, h, device, plane).start()

    def turn(slot, h, i, pages, span, plane, own):
        device = partner(h, i)
        attend((slot, h, device, pages, span))
        send_home(slot, h, device, plane, own & alone(h, i))

    far_pages = range(split)
    near_pages = range(1, live - 2)
    hub_pages = range(2, live - 1)
    top_pages = range(split, live)
    def stays_far(step):
        return lax.rem(partner(last, step), sub_size) == sub_size - 1

    def own_queries(h):
        q_local(h, own_recv.at[h]).start()
        for step in range(mates):
            if (step, mates - 1 - step)[h != 0]:
                q_remote(h, step, z, own_recv.at[h]).start()

    @pl.when(z == HUB)
    def _():
        hand_far()
        own_pages()
        pl.semaphore_wait(go, 1)
        exchange()
        own_queries(0)

    @pl.when((z == TOP) & (s == 0))
    def _():
        for h in range(per_core):
            hand_hub(pages_here, h, 1)

    @pl.when((z == TOP) & (s == 1))
    def _():
        hand_hub(1, 0, 2)

    @pl.when(z == TOP)
    def _():
        own_pages()
        exchange()
        for h in range(per_core):
            own_queries(h)

    @pl.when(z == FAR)
    def _():
        for h in range(per_core):
            recv = q_recv.at[FAR, h, mine]
            for step in range(mates):
                if h == 0 and step == OWN:
                    pl.semaphore_wait(go, 1)
                if h < last:
                    q_remote(h, step, HUB, recv, 0 if step < AHEAD else 1).start()
                else:
                    keep = stays_far(step)

                    @pl.when(jnp.logical_not(keep))
                    def _():
                        q_remote(h, step, HUB, recv).start()

                    @pl.when(keep)
                    def _():
                        if mates - 1 - step:
                            q_remote(h, step, FAR, recv).start()
                        else:
                            q_local(h, recv).start()

        settle(q_send.at[0], AHEAD)
        vouch(NEAR)

    @pl.when(z == NEAR)
    def _():
        for step in range(EARLY):
            q_remote(0, step, HUB, q_recv.at[NEAR, 0, mine]).start()
        pl.semaphore_wait(go, 2)
        for h in range(per_core):
            for step in range(mates):
                if h or step >= EARLY:
                    q_remote(h, step, HUB, q_recv.at[NEAR, h, mine]).start()

    counts_copy.wait()

    @pl.when((z == HUB) | ((z == FAR) & (s == sub_size - 1)))
    def _():
        span = span_of(FAR)
        h_low = jnp.where(z == FAR, last, 0)
        h_high = jnp.where((z == HUB) & (s == sub_size - 1), last, per_core)

        def step(n, carry):
            h, i = n // mates, n % mates

            @pl.when(i == 0)
            def _():
                kv_await(h, 0, split)

            @pl.when((n == WHEN) & (z == HUB))
            def _():
                own_queries(last)

            q_await(FAR, h, partner(h, i))
            turn(FAR, h, i, far_pages, span, FAR, z == FAR)
            return carry

        lax.fori_loop(h_low * mates, h_high * mates, step, 0)

    @pl.when(z == HUB)
    def _():
        @pl.when(s == sub_size - 1)
        def _():
            kv_await(last, 0, split)

        near_span, hub_span = span_of(NEAR), span_of(HUB)

        def near_task(n):
            h, i = n // mates, n % mates
            device = partner(h, i)
            q_await(NEAR, h, device)
            return NEAR, h, device, near_pages, near_span

        def own_task(n):
            h, i = n // mates, n % mates
            return HUB, h, partner(h, i), hub_pages, hub_span

        def near_home(n):
            h, i = n // mates, n % mates
            o_remote(NEAR, h, partner(h, i), NEAR).start()

        def own_home(n):
            h, i = n // mates, n % mates
            send_home(HUB, h, partner(h, i), HUB, alone(h, i))

        def ready(h):
            own_await(h)
            kv_await(h, split + pages_here, 1)

        def lead(n, carry):
            attend(near_task(n))
            near_home(n)
            return carry

        def both(n, carry):
            ahead = n + jnp.where(n < mates, 0, LAG)

            @pl.when(n == 0)
            def _():
                kv_await(0, split, pages_here)
                ready(0)

            @pl.when(n == mates)
            def _():
                kv_await(last, split, pages_here)
                lax.fori_loop(mates, mates + LAG, lead, 0)
                ready(last)

            attend(near_task(ahead), own_task(n))
            near_home(ahead)
            own_home(n)
            return carry

        lax.fori_loop(0, per_core * mates - LAG, both, 0)
        rest = range(per_core * mates - LAG, per_core * mates)
        attend(*[own_task(n) for n in rest])
        for n in rest:
            own_home(n)

    @pl.when(z == TOP)
    def _():
        span = span_of(TOP)

        def step(n, carry):
            h, i = n // mates, n % mates

            @pl.when(i == 0)
            def _():
                own_await(h)
                kv_await(h, split, split)

            turn(HUB, h, i, top_pages, span, TOP, True)

            return carry

        lax.fori_loop(0, per_core * mates, step, 0)

        @pl.when(s == 0)
        def _():
            settle_kv(2 * (pages_here * per_core * sub_size - 1), 1)
            pl.semaphore_signal(go, device_id={"sub": 1}, device_id_type=MESH)

        @pl.when(s == 1)
        def _():
            pl.semaphore_wait(go, 1)
            hand_hub(1, last, 2)

    def finals():
        settle(o_recv.at[0], per_core * mates)

    finals()

    @pl.when(z == HUB)
    def _():
        settle_kv(2 * pages_here * (per_core + 1))
        settle(o_send.at[NEAR], per_core * mates)

        @pl.when(s == 0)
        def _():
            settle(o_send.at[FAR], per_core * mates)

        @pl.when(s == 1)
        def _():
            settle(o_send.at[FAR], last * mates)

    @pl.when(z == TOP)
    def _():
        settle_kv(2 * pages_here * per_core)

        @pl.when(s == 0)
        def _():
            settle_kv(2, 2)

        @pl.when(s == 1)
        def _():
            settle_kv(2 * per_core * sub_size, 1)

    @pl.when(z >= HUB)
    def _():
        settle(q_send.at[1], per_core * (mates - 1))
        settle(o_send.at[HUB], per_core * (mates - 1))

    @pl.when(z == NEAR)
    def _():
        settle(q_send.at[1], per_core * mates)

    @pl.when((z == FAR) & (s == 0))
    def _():
        settle(q_send.at[1], per_core * mates - AHEAD)

    @pl.when((z == FAR) & (s == 1))
    def _():
        settle(q_send.at[1], per_core * mates - 1 - AHEAD)
        settle(o_send.at[FAR], mates - 1)


def served(queries, kv_cache, page_counts):
    ctx_size, sub_size = lax.axis_size("ctx"), lax.axis_size("sub")
    head_size = lax.axis_size("head")
    pages_here = kv_cache.shape[1] // PAGE
    mates = head_size * sub_size
    per_core = KVH // mates
    group = HQ // KVH
    live = pages_here * ctx_size * sub_size // 2
    tok_rows = queries.shape[0]
    slots = ctx_size - 1
    dma = pltpu.SemaphoreType.DMA
    chunk = (slots, per_core, mates, tok_rows, group * HD)
    return pl.pallas_call(
        functools.partial(serve_kernel, (head_size, sub_size, pages_here)),
        out_shape=jax.ShapeDtypeStruct(queries.shape, jnp.bfloat16),
        in_specs=[
            pl.BlockSpec(memory_space=pl.ANY),
            pl.BlockSpec(memory_space=pl.ANY),
            pl.BlockSpec(memory_space=pl.ANY),
        ],
        out_specs=pl.BlockSpec(memory_space=pl.ANY),
        scratch_shapes=[
            pltpu.SMEM((REQS,), jnp.int32),
            pltpu.VMEM((per_core, 2, live * PAGE, HD), jnp.bfloat16),
            pltpu.VMEM(chunk, jnp.bfloat16),
            pltpu.VMEM(chunk, jnp.bfloat16),
            pltpu.VMEM((group * tok_rows, (live - 3) * PAGE), jnp.float32),
            pltpu.VMEM((group * tok_rows, (live - 3) * PAGE), jnp.float32),
            dma((1,)),
            dma((2,)),
            dma((slots - 1, per_core, mates)),
            dma((per_core,)),
            dma((slots,)),
            dma((1,)),
            dma((3,)),
            dma((per_core, 3)),
            pltpu.SemaphoreType.REGULAR,
        ],
        compiler_params=pltpu.CompilerParams(
            collective_id=0, has_side_effects=True, vmem_limit_bytes=VMEM_LIMIT
        ),
    )(
        pltpu.with_memory_space_constraint(page_counts, pltpu.HBM),
        pltpu.with_memory_space_constraint(queries, pltpu.HBM),
        pltpu.with_memory_space_constraint(kv_cache, pltpu.HBM),
    )


def solution(mesh):
    specs = dict(
        mesh=mesh,
        in_specs=(
            P(("grp", "ctx", "head", "sub"), None),
            P(None, ("grp", "ctx", "sub"), "head"),
            P("grp"),
        ),
        out_specs=P(("grp", "ctx", "head", "sub"), None),
        check_vma=False,
    )

    def run(queries, kv_cache, page_counts):
        body = served if can_serve(mesh, kv_cache.shape[1]) else per_device
        return jax.shard_map(body, **specs)(queries, kv_cache, page_counts)

    return run
```

```python
import functools
import math

import jax
import jax.numpy as jnp
from jax import lax
from jax.experimental import pallas as pl
from jax.experimental.pallas import tpu as pltpu
from jax.sharding import PartitionSpec as P

HQ = 128
KVH = 8
HD = 128
REQS = 4
QR = 64
PAGE = 256
SPAN = 256


NEG = -1e30
MESH = pl.DeviceIdType.MESH
VMEM_LIMIT = 40000000
WHEN = 2
OWN = 2
LAG = 2
AHEAD = 3


def from_behind(array, axis, by):
    count = lax.axis_size(axis)
    pairs = [(i, i + by) for i in range(count) if 0 <= i + by < count]
    return lax.ppermute(array, axis, pairs)


def per_device(queries, kv_cache, page_counts):
    per_group = HQ // KVH
    local_heads = kv_cache.shape[2] // HD
    ctx_size = lax.axis_size("ctx")
    sub_size = lax.axis_size("sub")
    head_count = lax.axis_size("head")
    tok_rows = queries.shape[0]
    score_scale = HD ** (-0.5)
    regrouped = lax.all_to_all(queries, "head", split_axis=1, concat_axis=0, tiled=True)
    all_queries = lax.all_gather(regrouped, ("ctx", "sub"), axis=0, tiled=True)
    all_queries = all_queries.reshape(SPAN, local_heads, per_group, HD)
    page_ends = jnp.cumsum(page_counts)
    ctx_rows = SPAN // ctx_size
    offsets = jnp.arange(QR, dtype=jnp.int32)
    columns = jnp.arange(PAGE, dtype=jnp.int32)
    flat_index = lax.axis_index("ctx") * sub_size + lax.axis_index("sub")
    pages_here = kv_cache.shape[1] // PAGE
    base_pages = pages_here * ctx_size * sub_size // 2
    initial = (
        jnp.full((SPAN, local_heads, per_group), NEG, jnp.float32),
        jnp.zeros((SPAN, local_heads, per_group), jnp.float32),
        jnp.zeros((SPAN, local_heads, per_group, HD), jnp.float32),
    )
    half_rows = kv_cache.shape[1] // 2
    arrived = from_behind(kv_cache[:, half_rows:], "ctx", -(ctx_size // 2))
    is_lower = lax.axis_index("ctx") < ctx_size // 2
    source_flat = flat_index + ctx_size // 2 * sub_size
    working = jnp.where(is_lower, arrived, kv_cache[:, :half_rows])
    first_page = jnp.where(
        is_lower, source_flat * pages_here + pages_here // 2, flat_index * pages_here
    )
    page_total = working.shape[1] // PAGE

    def add_page(page_turn, running):
        page_index = first_page + page_turn
        relative = page_index - base_pages
        counted = jnp.sum((relative >= page_ends).astype(jnp.int32))
        request = jnp.where(relative < 0, REQS, counted)

        def update(partial_value):
            run_max, run_sum, run_out = partial_value
            request_id = jnp.minimum(request, REQS - 1)
            row_start = request_id * QR
            gathered = row_start + offsets
            within = gathered % ctx_rows
            ctx_block = gathered // ctx_rows
            sub_part = within // (head_count * tok_rows)
            head_part = within // tok_rows % head_count
            tok_part = within % tok_rows
            natural = ctx_block * ctx_rows + (head_part * sub_size + sub_part) * tok_rows + tok_part
            query_pos = (page_ends[request_id] + base_pages) * PAGE - QR + natural - row_start
            key_pos = page_index * PAGE + columns
            visible = key_pos[None, :] <= query_pos[:, None]
            page_keys = working[0].reshape(PAGE, local_heads, HD)
            page_values = working[1].reshape(PAGE, local_heads, HD)
            query_rows = lax.dynamic_slice_in_dim(all_queries, row_start, QR, 0)
            scores = (
                jnp.einsum(
                    "qkgd,pkd->qkgp", query_rows, page_keys, preferred_element_type=jnp.float32
                )
                * score_scale
            )
            scores = jnp.where(visible[:, None, None, :], scores, NEG)
            old_max = lax.dynamic_slice_in_dim(run_max, row_start, QR, 0)
            old_sum = lax.dynamic_slice_in_dim(run_sum, row_start, QR, 0)
            old_out = lax.dynamic_slice_in_dim(run_out, row_start, QR, 0)
            new_max = jnp.maximum(old_max, jnp.max(scores, axis=3))
            factor = jnp.exp(old_max - new_max)
            numerators = jnp.exp(scores - new_max[..., None])
            new_sum = old_sum * factor + jnp.sum(numerators, axis=3)
            product = jnp.einsum(
                "qkgp,pkd->qkgd",
                numerators.astype(jnp.bfloat16),
                page_values,
                preferred_element_type=jnp.float32,
            )
            new_out = old_out * factor[..., None] + product
            return (
                lax.dynamic_update_slice_in_dim(run_max, new_max, row_start, 0),
                lax.dynamic_update_slice_in_dim(run_sum, new_sum, row_start, 0),
                lax.dynamic_update_slice_in_dim(run_out, new_out, row_start, 0),
            )

        def unchanged(partial_value):
            return partial_value

        return lax.cond(request < REQS, update, unchanged, running)

    run_max, run_sum, run_out = lax.fori_loop(0, page_total, add_page, initial)
    share = SPAN // (ctx_size * sub_size)
    global_max = lax.pmax(run_max, ("ctx", "sub"))
    factor = jnp.exp(run_max - global_max)
    sums_here, outs_here = (
        lax.psum_scatter(
            (run_sum * factor).astype(jnp.bfloat16), ("ctx", "sub"), scatter_dimension=0, tiled=True
        ).astype(jnp.float32),
        lax.psum_scatter(
            (run_out * factor[..., None]).astype(jnp.bfloat16),
            ("ctx", "sub"),
            scatter_dimension=0,
            tiled=True,
        ).astype(jnp.float32),
    )
    finished = (outs_here / sums_here[..., None]).astype(jnp.bfloat16)
    finished = finished.reshape(share, local_heads * per_group * HD)
    return lax.all_to_all(finished, "head", split_axis=0, concat_axis=1, tiled=True)


FAR, NEAR, HUB, TOP = range(4)


def can_serve(mesh, rows):
    ctx_size, sub_size, head_size = mesh.shape["ctx"], mesh.shape["sub"], mesh.shape["head"]
    if ctx_size != REQS or SPAN // ctx_size != QR or sub_size != 2:
        return False
    pages_here = rows // (mesh.shape["grp"] * ctx_size * sub_size) // PAGE
    return pages_here == 2 and head_size == 2 and KVH == 2 * head_size * sub_size


def serve_kernel(
    sizes,
    counts_hbm,
    q_hbm,
    kv_hbm,
    out_ref,
    counts_ref,
    kvbuf,
    qbuf,
    obuf,
    sbuf,
    tbuf,
    counts_sem,
    q_send,
    q_recv,
    own_recv,
    o_send,
    o_recv,
    kv_send,
    kv_recv,
    go,
):
    head_size, sub_size, pages_here = sizes
    mates = head_size * sub_size
    per_core = KVH // mates
    group = HQ // KVH
    width = group * HD
    tok_rows = QR // mates
    rows = group * tok_rows
    split = pages_here * sub_size
    live = 2 * split
    z, x, s = lax.axis_index("ctx"), lax.axis_index("head"), lax.axis_index("sub")
    mine = x * sub_size + s
    slot_of = jnp.minimum(z, HUB)
    factor = HD ** (-0.5) * math.log2(math.e)

    def at(device, plane=None):
        place = {"head": device // sub_size, "sub": device % sub_size}
        if plane is not None:
            place["ctx"] = plane
        return place

    barrier = pltpu.get_barrier_semaphore()
    counts_copy = pltpu.make_async_copy(counts_hbm, counts_ref, counts_sem.at[0])
    counts_copy.start()

    def greet(place):
        pl.semaphore_signal(barrier, device_id=place, device_id_type=MESH)

    def greet_plane(plane):
        for device in range(mates):
            greet(at(device, plane))

    def greet_column(plane):
        for core in range(sub_size):
            greet({"ctx": plane, "sub": core})

    def greet_mates():
        for step in range(1, mates):
            greet(at(lax.rem(mine + step, mates)))

    def vouch(plane):
        pl.semaphore_signal(go, device_id={"ctx": plane}, device_id_type=MESH)

    @pl.when(z == HUB)
    def _():
        greet_column(NEAR)
        greet_column(FAR)
        greet_plane(TOP)
        pl.semaphore_wait(barrier, sub_size)

    @pl.when(z == TOP)
    def _():
        greet_mates()
        pl.semaphore_wait(barrier, 4 * mates - 1)
        vouch(HUB)
        vouch(FAR)
        vouch(NEAR)

    @pl.when(z == NEAR)
    def _():
        greet_plane(TOP)
        pl.semaphore_wait(barrier, sub_size)

    @pl.when(z == FAR)
    def _():
        greet_column(HUB)
        greet_plane(TOP)
        pl.semaphore_wait(barrier, sub_size)

    def partner(h, step):
        turned = jnp.where(h == 0, step, mates - 1 - step)
        far_x, far_s = turned // sub_size, turned % sub_size
        return lax.rem(x + far_x, head_size) * sub_size + lax.rem(s + far_s, sub_size)

    def alone(h, step):
        return jnp.where(h == 0, step, mates - 1 - step) == 0

    def cols(device, h):
        return pl.ds(pl.multiple_of((device * per_core + h) * width, width), width)

    def q_remote(h, step, plane, recv, part=1):
        other = partner(h, step)
        return pltpu.make_async_remote_copy(
            src_ref=q_hbm.at[:, cols(other, h)],
            dst_ref=qbuf.at[slot_of, h, mine],
            send_sem=q_send.at[part],
            recv_sem=recv,
            device_id=at(other, plane),
            device_id_type=MESH,
        )

    def q_local(h, recv):
        return pltpu.make_async_copy(q_hbm.at[:, cols(mine, h)], qbuf.at[slot_of, h, mine], recv)

    def q_await(slot, h, device):
        pltpu.make_async_copy(
            q_hbm.at[:, cols(0, 0)], qbuf.at[slot, h, device], q_recv.at[slot, h, device]
        ).wait()

    def own_await(h):
        pltpu.make_async_copy(obuf.at[HUB, h], qbuf.at[HUB, h], own_recv.at[h]).wait()

    def o_remote(slot, h, device, plane):
        return pltpu.make_async_remote_copy(
            src_ref=obuf.at[slot, h, device],
            dst_ref=out_ref.at[:, cols(mine, h)],
            send_sem=o_send.at[slot],
            recv_sem=o_recv.at[0],
            device_id=at(device, plane),
            device_id_type=MESH,
        )

    def o_local(slot, h):
        return pltpu.make_async_copy(
            obuf.at[slot, h, mine], out_ref.at[:, cols(mine, h)], o_recv.at[0]
        )

    def settle(sem, chunks):
        span = pl.ds(0, chunks * width)
        pltpu.make_async_copy(q_hbm.at[:, span], out_ref.at[:, span], sem).wait()

    def settle_kv(blocks, part=0):
        span = pl.ds(0, blocks * PAGE // (2 * per_core))
        pltpu.make_async_copy(kvbuf.at[:, :, span], kvbuf.at[:, :, span], kv_send.at[part]).wait()

    def kv_block(core, h, held, skip=0):
        return kv_hbm.at[
            :,
            pl.ds(skip * PAGE, held * PAGE),
            pl.ds(pl.multiple_of((core * per_core + h) * HD, HD), HD),
        ]

    def kv_place(h, p, held):
        return kvbuf.at[h, :, pl.ds(pl.multiple_of(p * PAGE, PAGE), held * PAGE)]

    here = (s + jnp.where(z == TOP, sub_size, 0)) * pages_here
    half = jnp.where(z == TOP, 1, 0)

    def kv_remote(h, core, held, target, recv, part=0, skip=0):
        return pltpu.make_async_remote_copy(
            src_ref=kv_block(core, h, held, skip),
            dst_ref=kv_place(h, here + skip, held),
            send_sem=kv_send.at[part],
            recv_sem=kv_recv.at[h, recv],
            device_id=target,
            device_id_type=MESH,
        )

    def kv_await(h, first, count):
        place = kv_place(h, first, count)
        recv = 0 if first < split else (1 if first == split else 2)
        pltpu.make_async_copy(place, place, kv_recv.at[h, recv]).wait()

    def own_pages():
        for h in range(per_core):
            pltpu.make_async_copy(
                kv_block(s, h, pages_here), kv_place(h, here, pages_here), kv_recv.at[h, half]
            ).start()

    def exchange():
        for h in range(per_core):
            kv_remote(h, 1 - s, pages_here, {"sub": 1 - s}, half).start()

    def hand_far():
        core = sub_size - 1
        kv_remote(
            per_core - 1, core, pages_here, {"ctx": FAR, "sub": core}, 0
        ).start()

    last = per_core - 1

    def hand_hub(held, h, recv):
        for core in reversed(range(sub_size)):
            target = {"ctx": HUB, "sub": core}
            if core == 0 and h == last and held > 1:
                kv_remote(h, core, held - 1, target, recv, 1).start()
                kv_remote(h, core, 1, target, recv, 2, held - 1).start()
            else:
                kv_remote(h, core, held, target, recv, 1).start()

    def span_of(r):
        first, count = jnp.int32(0), jnp.int32(0)
        for i in range(REQS):
            if i < r:
                first = first + counts_ref[i]
            if i == r:
                count = counts_ref[i]
        return first * PAGE, (first + count) * PAGE - QR

    token = lax.broadcasted_iota(jnp.int32, (tok_rows, PAGE), 0)
    column = lax.broadcasted_iota(jnp.int32, (tok_rows, PAGE), 1)

    def score(task, room):
        slot, h, device, pages, (first_pos, query_base) = task
        last_seen = query_base + device * tok_rows + token
        query = jnp.concatenate(
            [qbuf[slot, h, device, :, j * HD : (j + 1) * HD] for j in range(group)], axis=0
        )
        top = jnp.full((rows, HD), NEG, jnp.float32)
        for n, p in enumerate(pages):
            keys = kvbuf[h, 0, p * PAGE : (p + 1) * PAGE, :]
            pos = p * PAGE + column
            bias = jnp.where((pos >= first_pos) & (pos <= last_seen), 0.0, NEG)
            scores = lax.dot_general(
                query, keys, (((1,), (1,)), ((), ())), preferred_element_type=jnp.float32
            )
            scores = scores.reshape(group, tok_rows, PAGE) + bias[None]
            scores = scores.reshape(rows, PAGE)
            room[:, n * PAGE : (n + 1) * PAGE] = scores
            for c in range(PAGE // HD):
                top = jnp.maximum(top, scores[:, c * HD : (c + 1) * HD])
        return top

    def weigh(task, room, top):
        slot, h, device, pages, _ = task
        top = jnp.broadcast_to(jnp.max(top, axis=1, keepdims=True), (rows, HD))
        total = jnp.zeros((rows, HD), jnp.float32)
        summed = jnp.zeros((rows, HD), jnp.float32)
        for n, p in enumerate(pages):
            parts = []
            for c in range(PAGE // HD):
                low = n * PAGE + c * HD
                parts.append(jnp.exp2((room[:, low : low + HD] - top) * factor))
                total = total + parts[-1]
            weights = jnp.concatenate([part.astype(jnp.bfloat16) for part in parts], axis=1)
            values = kvbuf[h, 1, p * PAGE : (p + 1) * PAGE, :]
            summed = summed + jnp.dot(weights, values, preferred_element_type=jnp.float32)
        done = summed / jnp.sum(total, axis=1, keepdims=True)
        done = done.astype(jnp.bfloat16)
        for j in range(group):
            obuf[slot, h, device, :, j * HD : (j + 1) * HD] = done[
                j * tok_rows : (j + 1) * tok_rows, :
            ]

    def attend(*tasks, then=None):
        rooms = (sbuf, tbuf)[: len(tasks)]
        tops = [score(task, room) for task, room in zip(tasks, rooms)]
        for task, room, top in zip(tasks, rooms, tops):
            weigh(task, room, top)
            if then is not None:
                then()
                then = None

    def send_home(slot, h, device, plane, stays):
        @pl.when(stays)
        def _():
            o_local(slot, h).start()

        @pl.when(jnp.logical_not(stays))
        def _():
            o_remote(slot, h, device, plane).start()

    def turn(slot, h, i, pages, span, plane, own):
        device = partner(h, i)
        attend((slot, h, device, pages, span))
        send_home(slot, h, device, plane, own & alone(h, i))

    far_pages = range(split)
    near_pages = range(1, live - 2)
    hub_pages = range(2, live - 1)
    top_pages = range(split, live)
    def stays_far(step):
        return lax.rem(partner(last, step), sub_size) == sub_size - 1

    def own_queries(h):
        q_local(h, own_recv.at[h]).start()
        for step in range(mates):
            if (step, mates - 1 - step)[h != 0]:
                q_remote(h, step, z, own_recv.at[h]).start()

    @pl.when(z == HUB)
    def _():
        hand_far()
        own_pages()
        pl.semaphore_wait(go, 1)
        exchange()
        own_queries(0)

    @pl.when((z == TOP) & (s == 0))
    def _():
        for h in range(per_core):
            hand_hub(pages_here, h, 1)

    @pl.when(z == TOP)
    def _():
        own_pages()
        exchange()
        for h in range(per_core):
            own_queries(h)

    @pl.when(z == FAR)
    def _():
        for h in range(per_core):
            recv = q_recv.at[FAR, h, mine]
            for step in range(mates):
                if h == 0 and step == OWN:
                    pl.semaphore_wait(go, 1)
                if h < last:
                    q_remote(h, step, HUB, recv, 0 if step < AHEAD else 1).start()
                else:
                    keep = stays_far(step)

                    @pl.when(jnp.logical_not(keep))
                    def _():
                        q_remote(h, step, HUB, recv).start()

                    @pl.when(keep)
                    def _():
                        if mates - 1 - step:
                            q_remote(h, step, FAR, recv).start()
                        else:
                            q_local(h, recv).start()

        settle(q_send.at[0], AHEAD)
        vouch(NEAR)

    @pl.when(z == NEAR)
    def _():
        @pl.when(s == 1)
        def _():
            q_remote(0, 0, HUB, q_recv.at[NEAR, 0, mine]).start()

        pl.semaphore_wait(go, 2)

        @pl.when(s == 0)
        def _():
            q_remote(0, 0, HUB, q_recv.at[NEAR, 0, mine]).start()

        for h in range(per_core):
            for step in range(mates):
                if h or step:
                    q_remote(h, step, HUB, q_recv.at[NEAR, h, mine]).start()

    counts_copy.wait()
    near_span, hub_span = span_of(NEAR), span_of(HUB)

    def near_task(n):
        h, i = n // mates, n % mates
        device = partner(h, i)
        q_await(NEAR, h, device)
        return NEAR, h, device, near_pages, near_span

    def own_task(n):
        h, i = n // mates, n % mates
        return HUB, h, partner(h, i), hub_pages, hub_span

    def near_home(n):
        h, i = n // mates, n % mates
        o_remote(NEAR, h, partner(h, i), NEAR).start()

    def own_home(n):
        h, i = n // mates, n % mates
        send_home(HUB, h, partner(h, i), HUB, alone(h, i))

    def ready(h):
        own_await(h)
        kv_await(h, split + pages_here, 1)

    def lead(n, carry):
        attend(near_task(n))
        near_home(n)
        return carry

    @pl.when((z == HUB) | ((z == FAR) & (s == sub_size - 1)))
    def _():
        span = span_of(FAR)
        h_low = jnp.where(z == FAR, last, 0)
        h_high = jnp.where((z == HUB) & (s == sub_size - 1), last, per_core)

        def step(n, carry):
            h, i = n // mates, n % mates

            @pl.when(i == 0)
            def _():
                kv_await(h, 0, split)

            @pl.when((n == WHEN) & (z == HUB))
            def _():
                own_queries(last)

            @pl.when((n == mates - 1) & (z == HUB) & (s == 1))
            def _():
                kv_await(0, split, pages_here)
                lead(0, 0)

            q_await(FAR, h, partner(h, i))
            turn(FAR, h, i, far_pages, span, FAR, z == FAR)
            return carry

        lax.fori_loop(h_low * mates, h_high * mates, step, 0)

    @pl.when(z == HUB)
    def _():
        @pl.when(s == sub_size - 1)
        def _():
            kv_await(last, 0, split)

        def both(n, carry):
            ahead = n + jnp.where(n < mates, s, LAG)

            @pl.when((n == 0) & (s == 0))
            def _():
                kv_await(0, split, pages_here)

            @pl.when(n == 0)
            def _():
                ready(0)

            @pl.when(n == mates - s)
            def _():
                kv_await(last, split, pages_here)

            @pl.when(n == mates)
            def _():
                lax.fori_loop(mates + s, mates + LAG, lead, 0)
                ready(last)

            attend(near_task(ahead), own_task(n), then=lambda: near_home(ahead))
            own_home(n)
            return carry

        lax.fori_loop(0, per_core * mates - LAG, both, 0)
        rest = range(per_core * mates - LAG, per_core * mates)
        attend(*[own_task(n) for n in rest])
        for n in rest:
            own_home(n)

    @pl.when(z == TOP)
    def _():
        span = span_of(TOP)

        def step(n, carry):
            h, i = n // mates, n % mates

            @pl.when(i == 0)
            def _():
                own_await(h)
                kv_await(h, split, split)

            @pl.when((n == 0) & (s == 1))
            def _():
                hand_hub(1, 0, 2)

            turn(HUB, h, i, top_pages, span, TOP, True)

            return carry

        lax.fori_loop(0, per_core * mates, step, 0)

        @pl.when(s == 0)
        def _():
            settle_kv(2 * (pages_here * per_core * sub_size - 1), 1)
            pl.semaphore_signal(go, device_id={"sub": 1}, device_id_type=MESH)

        @pl.when(s == 1)
        def _():
            pl.semaphore_wait(go, 1)
            hand_hub(1, last, 2)

    def finals():
        settle(o_recv.at[0], per_core * mates)

    finals()

    @pl.when(z == HUB)
    def _():
        settle_kv(2 * pages_here * (per_core + 1))
        settle(o_send.at[NEAR], per_core * mates)

        @pl.when(s == 0)
        def _():
            settle(o_send.at[FAR], per_core * mates)

        @pl.when(s == 1)
        def _():
            settle(o_send.at[FAR], last * mates)

    @pl.when(z == TOP)
    def _():
        settle_kv(2 * pages_here * per_core)

        @pl.when(s == 0)
        def _():
            settle_kv(2, 2)

        @pl.when(s == 1)
        def _():
            settle_kv(2 * per_core * sub_size, 1)

    @pl.when(z >= HUB)
    def _():
        settle(q_send.at[1], per_core * (mates - 1))
        settle(o_send.at[HUB], per_core * (mates - 1))

    @pl.when(z == NEAR)
    def _():
        settle(q_send.at[1], per_core * mates)

    @pl.when((z == FAR) & (s == 0))
    def _():
        settle(q_send.at[1], per_core * mates - AHEAD)

    @pl.when((z == FAR) & (s == 1))
    def _():
        settle(q_send.at[1], per_core * mates - 1 - AHEAD)
        settle(o_send.at[FAR], mates - 1)


def served(queries, kv_cache, page_counts):
    ctx_size, sub_size = lax.axis_size("ctx"), lax.axis_size("sub")
    head_size = lax.axis_size("head")
    pages_here = kv_cache.shape[1] // PAGE
    mates = head_size * sub_size
    per_core = KVH // mates
    group = HQ // KVH
    live = pages_here * ctx_size * sub_size // 2
    tok_rows = queries.shape[0]
    slots = ctx_size - 1
    dma = pltpu.SemaphoreType.DMA
    chunk = (slots, per_core, mates, tok_rows, group * HD)
    return pl.pallas_call(
        functools.partial(serve_kernel, (head_size, sub_size, pages_here)),
        out_shape=jax.ShapeDtypeStruct(queries.shape, jnp.bfloat16),
        in_specs=[
            pl.BlockSpec(memory_space=pl.ANY),
            pl.BlockSpec(memory_space=pl.ANY),
            pl.BlockSpec(memory_space=pl.ANY),
        ],
        out_specs=pl.BlockSpec(memory_space=pl.ANY),
        scratch_shapes=[
            pltpu.SMEM((REQS,), jnp.int32),
            pltpu.VMEM((per_core, 2, live * PAGE, HD), jnp.bfloat16),
            pltpu.VMEM(chunk, jnp.bfloat16),
            pltpu.VMEM(chunk, jnp.bfloat16),
            pltpu.VMEM((group * tok_rows, (live - 3) * PAGE), jnp.float32),
            pltpu.VMEM((group * tok_rows, (live - 3) * PAGE), jnp.float32),
            dma((1,)),
            dma((2,)),
            dma((slots - 1, per_core, mates)),
            dma((per_core,)),
            dma((slots,)),
            dma((1,)),
            dma((3,)),
            dma((per_core, 3)),
            pltpu.SemaphoreType.REGULAR,
        ],
        compiler_params=pltpu.CompilerParams(
            collective_id=0, has_side_effects=True, vmem_limit_bytes=VMEM_LIMIT
        ),
    )(
        pltpu.with_memory_space_constraint(page_counts, pltpu.HBM),
        pltpu.with_memory_space_constraint(queries, pltpu.HBM),
        pltpu.with_memory_space_constraint(kv_cache, pltpu.HBM),
    )


def solution(mesh):
    specs = dict(
        mesh=mesh,
        in_specs=(
            P(("grp", "ctx", "head", "sub"), None),
            P(None, ("grp", "ctx", "sub"), "head"),
            P("grp"),
        ),
        out_specs=P(("grp", "ctx", "head", "sub"), None),
        check_vma=False,
    )

    def run(queries, kv_cache, page_counts):
        body = served if can_serve(mesh, kv_cache.shape[1]) else per_device
        return jax.shard_map(body, **specs)(queries, kv_cache, page_counts)

    return run
```

```python
import functools
import math

import jax
import jax.numpy as jnp
from jax import lax
from jax.experimental import pallas as pl
from jax.experimental.pallas import tpu as pltpu
from jax.sharding import PartitionSpec as P

HQ = 128
KVH = 8
HD = 128
REQS = 4
QR = 64
PAGE = 256
SPAN = 256


NEG = -1e30
MESH = pl.DeviceIdType.MESH
VMEM_LIMIT = 40000000
WHEN = 2
OWN = 2
LAG = 2
AHEAD = 3


def from_behind(array, axis, by):
    count = lax.axis_size(axis)
    pairs = [(i, i + by) for i in range(count) if 0 <= i + by < count]
    return lax.ppermute(array, axis, pairs)


def per_device(queries, kv_cache, page_counts):
    per_group = HQ // KVH
    local_heads = kv_cache.shape[2] // HD
    ctx_size = lax.axis_size("ctx")
    sub_size = lax.axis_size("sub")
    head_count = lax.axis_size("head")
    tok_rows = queries.shape[0]
    score_scale = HD ** (-0.5)
    regrouped = lax.all_to_all(queries, "head", split_axis=1, concat_axis=0, tiled=True)
    all_queries = lax.all_gather(regrouped, ("ctx", "sub"), axis=0, tiled=True)
    all_queries = all_queries.reshape(SPAN, local_heads, per_group, HD)
    page_ends = jnp.cumsum(page_counts)
    ctx_rows = SPAN // ctx_size
    offsets = jnp.arange(QR, dtype=jnp.int32)
    columns = jnp.arange(PAGE, dtype=jnp.int32)
    flat_index = lax.axis_index("ctx") * sub_size + lax.axis_index("sub")
    pages_here = kv_cache.shape[1] // PAGE
    base_pages = pages_here * ctx_size * sub_size // 2
    initial = (
        jnp.full((SPAN, local_heads, per_group), NEG, jnp.float32),
        jnp.zeros((SPAN, local_heads, per_group), jnp.float32),
        jnp.zeros((SPAN, local_heads, per_group, HD), jnp.float32),
    )
    half_rows = kv_cache.shape[1] // 2
    arrived = from_behind(kv_cache[:, half_rows:], "ctx", -(ctx_size // 2))
    is_lower = lax.axis_index("ctx") < ctx_size // 2
    source_flat = flat_index + ctx_size // 2 * sub_size
    working = jnp.where(is_lower, arrived, kv_cache[:, :half_rows])
    first_page = jnp.where(
        is_lower, source_flat * pages_here + pages_here // 2, flat_index * pages_here
    )
    page_total = working.shape[1] // PAGE

    def add_page(page_turn, running):
        page_index = first_page + page_turn
        relative = page_index - base_pages
        counted = jnp.sum((relative >= page_ends).astype(jnp.int32))
        request = jnp.where(relative < 0, REQS, counted)

        def update(partial_value):
            run_max, run_sum, run_out = partial_value
            request_id = jnp.minimum(request, REQS - 1)
            row_start = request_id * QR
            gathered = row_start + offsets
            within = gathered % ctx_rows
            ctx_block = gathered // ctx_rows
            sub_part = within // (head_count * tok_rows)
            head_part = within // tok_rows % head_count
            tok_part = within % tok_rows
            natural = ctx_block * ctx_rows + (head_part * sub_size + sub_part) * tok_rows + tok_part
            query_pos = (page_ends[request_id] + base_pages) * PAGE - QR + natural - row_start
            key_pos = page_index * PAGE + columns
            visible = key_pos[None, :] <= query_pos[:, None]
            page_keys = working[0].reshape(PAGE, local_heads, HD)
            page_values = working[1].reshape(PAGE, local_heads, HD)
            query_rows = lax.dynamic_slice_in_dim(all_queries, row_start, QR, 0)
            scores = (
                jnp.einsum(
                    "qkgd,pkd->qkgp", query_rows, page_keys, preferred_element_type=jnp.float32
                )
                * score_scale
            )
            scores = jnp.where(visible[:, None, None, :], scores, NEG)
            old_max = lax.dynamic_slice_in_dim(run_max, row_start, QR, 0)
            old_sum = lax.dynamic_slice_in_dim(run_sum, row_start, QR, 0)
            old_out = lax.dynamic_slice_in_dim(run_out, row_start, QR, 0)
            new_max = jnp.maximum(old_max, jnp.max(scores, axis=3))
            factor = jnp.exp(old_max - new_max)
            numerators = jnp.exp(scores - new_max[..., None])
            new_sum = old_sum * factor + jnp.sum(numerators, axis=3)
            product = jnp.einsum(
                "qkgp,pkd->qkgd",
                numerators.astype(jnp.bfloat16),
                page_values,
                preferred_element_type=jnp.float32,
            )
            new_out = old_out * factor[..., None] + product
            return (
                lax.dynamic_update_slice_in_dim(run_max, new_max, row_start, 0),
                lax.dynamic_update_slice_in_dim(run_sum, new_sum, row_start, 0),
                lax.dynamic_update_slice_in_dim(run_out, new_out, row_start, 0),
            )

        def unchanged(partial_value):
            return partial_value

        return lax.cond(request < REQS, update, unchanged, running)

    run_max, run_sum, run_out = lax.fori_loop(0, page_total, add_page, initial)
    share = SPAN // (ctx_size * sub_size)
    global_max = lax.pmax(run_max, ("ctx", "sub"))
    factor = jnp.exp(run_max - global_max)
    sums_here, outs_here = (
        lax.psum_scatter(
            (run_sum * factor).astype(jnp.bfloat16), ("ctx", "sub"), scatter_dimension=0, tiled=True
        ).astype(jnp.float32),
        lax.psum_scatter(
            (run_out * factor[..., None]).astype(jnp.bfloat16),
            ("ctx", "sub"),
            scatter_dimension=0,
            tiled=True,
        ).astype(jnp.float32),
    )
    finished = (outs_here / sums_here[..., None]).astype(jnp.bfloat16)
    finished = finished.reshape(share, local_heads * per_group * HD)
    return lax.all_to_all(finished, "head", split_axis=0, concat_axis=1, tiled=True)


FAR, NEAR, HUB, TOP = range(4)


def can_serve(mesh, rows):
    ctx_size, sub_size, head_size = mesh.shape["ctx"], mesh.shape["sub"], mesh.shape["head"]
    if ctx_size != REQS or SPAN // ctx_size != QR or sub_size != 2:
        return False
    pages_here = rows // (mesh.shape["grp"] * ctx_size * sub_size) // PAGE
    return pages_here == 2 and head_size == 2 and KVH == 2 * head_size * sub_size


def serve_kernel(
    sizes,
    counts_hbm,
    q_hbm,
    kv_hbm,
    out_ref,
    counts_ref,
    kvbuf,
    qbuf,
    obuf,
    sbuf,
    tbuf,
    counts_sem,
    q_send,
    q_recv,
    own_recv,
    o_send,
    o_recv,
    kv_send,
    kv_recv,
    go,
):
    head_size, sub_size, pages_here = sizes
    mates = head_size * sub_size
    per_core = KVH // mates
    group = HQ // KVH
    width = group * HD
    tok_rows = QR // mates
    rows = group * tok_rows
    split = pages_here * sub_size
    live = 2 * split
    z, x, s = lax.axis_index("ctx"), lax.axis_index("head"), lax.axis_index("sub")
    mine = x * sub_size + s
    slot_of = jnp.minimum(z, HUB)
    factor = HD ** (-0.5) * math.log2(math.e)

    def at(device, plane=None):
        place = {"head": device // sub_size, "sub": device % sub_size}
        if plane is not None:
            place["ctx"] = plane
        return place

    barrier = pltpu.get_barrier_semaphore()
    counts_copy = pltpu.make_async_copy(counts_hbm, counts_ref, counts_sem.at[0])
    counts_copy.start()

    def greet(place):
        pl.semaphore_signal(barrier, device_id=place, device_id_type=MESH)

    def greet_plane(plane):
        for device in range(mates):
            greet(at(device, plane))

    def greet_column(plane):
        for core in range(sub_size):
            greet({"ctx": plane, "sub": core})

    def greet_mates():
        for step in range(1, mates):
            greet(at(lax.rem(mine + step, mates)))

    def vouch(plane):
        pl.semaphore_signal(go, device_id={"ctx": plane}, device_id_type=MESH)

    @pl.when(z == HUB)
    def _():
        greet_column(FAR)
        greet_column(NEAR)
        greet_plane(TOP)
        pl.semaphore_wait(barrier, sub_size)

    @pl.when(z == TOP)
    def _():
        greet_mates()
        pl.semaphore_wait(barrier, 4 * mates - 1)
        vouch(HUB)
        vouch(FAR)
        vouch(NEAR)

    @pl.when(z == NEAR)
    def _():
        greet_plane(TOP)
        pl.semaphore_wait(barrier, sub_size)

    @pl.when(z == FAR)
    def _():
        greet_column(HUB)
        greet_plane(TOP)
        pl.semaphore_wait(barrier, sub_size)

    def partner(h, step):
        turned = jnp.where(h == 0, step, mates - 1 - step)
        far_x, far_s = turned // sub_size, turned % sub_size
        return lax.rem(x + far_x, head_size) * sub_size + lax.rem(s + far_s, sub_size)

    def alone(h, step):
        return jnp.where(h == 0, step, mates - 1 - step) == 0

    def cols(device, h):
        return pl.ds(pl.multiple_of((device * per_core + h) * width, width), width)

    def q_remote(h, step, plane, recv, part=1):
        other = partner(h, step)
        return pltpu.make_async_remote_copy(
            src_ref=q_hbm.at[:, cols(other, h)],
            dst_ref=qbuf.at[slot_of, h, mine],
            send_sem=q_send.at[part],
            recv_sem=recv,
            device_id=at(other, plane),
            device_id_type=MESH,
        )

    def q_local(h, recv):
        return pltpu.make_async_copy(q_hbm.at[:, cols(mine, h)], qbuf.at[slot_of, h, mine], recv)

    def q_await(slot, h, device):
        pltpu.make_async_copy(
            q_hbm.at[:, cols(0, 0)], qbuf.at[slot, h, device], q_recv.at[slot, h, device]
        ).wait()

    def own_await(h):
        pltpu.make_async_copy(obuf.at[HUB, h], qbuf.at[HUB, h], own_recv.at[h]).wait()

    def o_remote(slot, h, device, plane):
        return pltpu.make_async_remote_copy(
            src_ref=obuf.at[slot, h, device],
            dst_ref=out_ref.at[:, cols(mine, h)],
            send_sem=o_send.at[slot],
            recv_sem=o_recv.at[0],
            device_id=at(device, plane),
            device_id_type=MESH,
        )

    def o_local(slot, h):
        return pltpu.make_async_copy(
            obuf.at[slot, h, mine], out_ref.at[:, cols(mine, h)], o_recv.at[0]
        )

    def settle(sem, chunks):
        span = pl.ds(0, chunks * width)
        pltpu.make_async_copy(q_hbm.at[:, span], out_ref.at[:, span], sem).wait()

    def settle_kv(blocks, part=0):
        span = pl.ds(0, blocks * PAGE // (2 * per_core))
        pltpu.make_async_copy(kvbuf.at[:, :, span], kvbuf.at[:, :, span], kv_send.at[part]).wait()

    def kv_block(core, h, held, skip=0):
        return kv_hbm.at[
            :,
            pl.ds(skip * PAGE, held * PAGE),
            pl.ds(pl.multiple_of((core * per_core + h) * HD, HD), HD),
        ]

    def kv_place(h, p, held):
        return kvbuf.at[h, :, pl.ds(pl.multiple_of(p * PAGE, PAGE), held * PAGE)]

    here = (s + jnp.where(z == TOP, sub_size, 0)) * pages_here
    half = jnp.where(z == TOP, 1, 0)

    def kv_remote(h, core, held, target, recv, part=0, skip=0):
        return pltpu.make_async_remote_copy(
            src_ref=kv_block(core, h, held, skip),
            dst_ref=kv_place(h, here + skip, held),
            send_sem=kv_send.at[part],
            recv_sem=kv_recv.at[h, recv],
            device_id=target,
            device_id_type=MESH,
        )

    def kv_await(h, first, count):
        place = kv_place(h, first, count)
        recv = 0 if first < split else (1 if first == split else 2)
        pltpu.make_async_copy(place, place, kv_recv.at[h, recv]).wait()

    def own_pages():
        for h in range(per_core):
            pltpu.make_async_copy(
                kv_block(s, h, pages_here), kv_place(h, here, pages_here), kv_recv.at[h, half]
            ).start()

    def exchange():
        for h in range(per_core):
            kv_remote(h, 1 - s, pages_here, {"sub": 1 - s}, half).start()

    def hand_far():
        core = sub_size - 1
        kv_remote(
            per_core - 1, core, pages_here, {"ctx": FAR, "sub": core}, 0
        ).start()

    last = per_core - 1

    def hand_hub(held, h, recv):
        for core in reversed(range(sub_size)):
            target = {"ctx": HUB, "sub": core}
            if core == 0 and h == last and held > 1:
                kv_remote(h, core, held - 1, target, recv, 1).start()
                kv_remote(h, core, 1, target, recv, 2, held - 1).start()
            else:
                kv_remote(h, core, held, target, recv, 1).start()

    def span_of(r):
        first, count = jnp.int32(0), jnp.int32(0)
        for i in range(REQS):
            if i < r:
                first = first + counts_ref[i]
            if i == r:
                count = counts_ref[i]
        return first * PAGE, (first + count) * PAGE - QR

    token = lax.broadcasted_iota(jnp.int32, (tok_rows, PAGE), 0)
    column = lax.broadcasted_iota(jnp.int32, (tok_rows, PAGE), 1)

    def score(task, room):
        slot, h, device, pages, (first_pos, query_base) = task
        last_seen = query_base + device * tok_rows + token
        query = jnp.concatenate(
            [qbuf[slot, h, device, :, j * HD : (j + 1) * HD] for j in range(group)], axis=0
        )
        top = jnp.full((rows, HD), NEG, jnp.float32)
        for n, p in enumerate(pages):
            keys = kvbuf[h, 0, p * PAGE : (p + 1) * PAGE, :]
            pos = p * PAGE + column
            bias = jnp.where((pos >= first_pos) & (pos <= last_seen), 0.0, NEG)
            scores = lax.dot_general(
                query, keys, (((1,), (1,)), ((), ())), preferred_element_type=jnp.float32
            )
            scores = scores.reshape(group, tok_rows, PAGE) + bias[None]
            scores = scores.reshape(rows, PAGE)
            room[:, n * PAGE : (n + 1) * PAGE] = scores
            for c in range(PAGE // HD):
                top = jnp.maximum(top, scores[:, c * HD : (c + 1) * HD])
        return top

    def weigh(task, room, top):
        slot, h, device, pages, _ = task
        top = jnp.broadcast_to(jnp.max(top, axis=1, keepdims=True), (rows, HD))
        total = jnp.zeros((rows, HD), jnp.float32)
        summed = jnp.zeros((rows, HD), jnp.float32)
        for n, p in enumerate(pages):
            parts = []
            for c in range(PAGE // HD):
                low = n * PAGE + c * HD
                parts.append(jnp.exp2((room[:, low : low + HD] - top) * factor))
                total = total + parts[-1]
            weights = jnp.concatenate([part.astype(jnp.bfloat16) for part in parts], axis=1)
            values = kvbuf[h, 1, p * PAGE : (p + 1) * PAGE, :]
            summed = summed + jnp.dot(weights, values, preferred_element_type=jnp.float32)
        done = summed / jnp.sum(total, axis=1, keepdims=True)
        done = done.astype(jnp.bfloat16)
        for j in range(group):
            obuf[slot, h, device, :, j * HD : (j + 1) * HD] = done[
                j * tok_rows : (j + 1) * tok_rows, :
            ]

    def attend(*tasks, then=None):
        rooms = (sbuf, tbuf)[: len(tasks)]
        tops = [score(task, room) for task, room in zip(tasks, rooms)]
        for task, room, top in zip(tasks, rooms, tops):
            weigh(task, room, top)
            if then is not None:
                then()
                then = None

    def send_home(slot, h, device, plane, stays):
        @pl.when(stays)
        def _():
            o_local(slot, h).start()

        @pl.when(jnp.logical_not(stays))
        def _():
            o_remote(slot, h, device, plane).start()

    def turn(slot, h, i, pages, span, plane, own):
        device = partner(h, i)
        attend((slot, h, device, pages, span))
        send_home(slot, h, device, plane, own & alone(h, i))

    far_pages = range(split)
    near_pages = range(1, live - 2)
    hub_pages = range(2, live - 1)
    top_pages = range(split, live)
    def stays_far(step):
        return lax.rem(partner(last, step), sub_size) == sub_size - 1

    def own_queries(h):
        q_local(h, own_recv.at[h]).start()
        for step in range(mates):
            if (step, mates - 1 - step)[h != 0]:
                q_remote(h, step, z, own_recv.at[h]).start()

    @pl.when(z == HUB)
    def _():
        hand_far()
        own_pages()
        pl.semaphore_wait(go, 1)
        exchange()
        own_queries(0)

    @pl.when((z == TOP) & (s == 0))
    def _():
        for h in range(per_core):
            hand_hub(pages_here, h, 1)

    @pl.when(z == TOP)
    def _():
        own_pages()
        exchange()
        for h in range(per_core):
            own_queries(h)

    @pl.when(z == FAR)
    def _():
        for h in range(per_core):
            recv = q_recv.at[FAR, h, mine]
            for step in range(mates):
                if h == 0 and step == OWN:
                    pl.semaphore_wait(go, 1)
                if h < last:
                    q_remote(h, step, HUB, recv, 0 if step < AHEAD else 1).start()
                else:
                    keep = stays_far(step)

                    @pl.when(jnp.logical_not(keep))
                    def _():
                        q_remote(h, step, HUB, recv).start()

                    @pl.when(keep)
                    def _():
                        if mates - 1 - step:
                            q_remote(h, step, FAR, recv).start()
                        else:
                            q_local(h, recv).start()

        settle(q_send.at[0], AHEAD)
        vouch(NEAR)

    @pl.when(z == NEAR)
    def _():
        @pl.when(s == 1)
        def _():
            q_remote(0, 0, HUB, q_recv.at[NEAR, 0, mine]).start()

        pl.semaphore_wait(go, 2)

        @pl.when(s == 0)
        def _():
            q_remote(0, 0, HUB, q_recv.at[NEAR, 0, mine]).start()

        for h in range(per_core):
            for step in range(mates):
                if h or step:
                    q_remote(h, step, HUB, q_recv.at[NEAR, h, mine]).start()

    counts_copy.wait()
    near_span, hub_span = span_of(NEAR), span_of(HUB)

    def near_task(n):
        h, i = n // mates, n % mates
        device = partner(h, i)
        q_await(NEAR, h, device)
        return NEAR, h, device, near_pages, near_span

    def own_task(n):
        h, i = n // mates, n % mates
        return HUB, h, partner(h, i), hub_pages, hub_span

    def near_home(n):
        h, i = n // mates, n % mates
        o_remote(NEAR, h, partner(h, i), NEAR).start()

    def own_home(n):
        h, i = n // mates, n % mates
        send_home(HUB, h, partner(h, i), HUB, alone(h, i))

    def ready(h):
        own_await(h)
        kv_await(h, split + pages_here, 1)

    def lead(n, carry):
        attend(near_task(n))
        near_home(n)
        return carry

    @pl.when((z == HUB) | ((z == FAR) & (s == sub_size - 1)))
    def _():
        span = span_of(FAR)
        h_low = jnp.where(z == FAR, last, 0)
        h_high = jnp.where((z == HUB) & (s == sub_size - 1), last, per_core)

        def step(n, carry):
            h, i = n // mates, n % mates

            @pl.when(i == 0)
            def _():
                kv_await(h, 0, split)

            @pl.when((n == WHEN) & (z == HUB))
            def _():
                own_queries(last)

            @pl.when((n == mates - 1) & (z == HUB) & (s == 1))
            def _():
                kv_await(0, split, pages_here)
                lead(0, 0)

            q_await(FAR, h, partner(h, i))
            turn(FAR, h, i, far_pages, span, FAR, z == FAR)
            return carry

        lax.fori_loop(h_low * mates, h_high * mates, step, 0)

    @pl.when(z == HUB)
    def _():
        @pl.when(s == sub_size - 1)
        def _():
            kv_await(last, 0, split)

        def both(n, carry):
            ahead = n + jnp.where(n < mates, s, LAG)

            @pl.when((n == 0) & (s == 0))
            def _():
                kv_await(0, split, pages_here)

            @pl.when(n == 0)
            def _():
                ready(0)

            @pl.when(n == mates - s)
            def _():
                kv_await(last, split, pages_here)

            @pl.when(n == mates)
            def _():
                lax.fori_loop(mates + s, mates + LAG, lead, 0)
                ready(last)

            attend(near_task(ahead), own_task(n), then=lambda: near_home(ahead))
            own_home(n)
            return carry

        lax.fori_loop(0, per_core * mates - LAG, both, 0)
        rest = range(per_core * mates - LAG, per_core * mates)
        attend(*[own_task(n) for n in rest])
        for n in rest:
            own_home(n)

    @pl.when(z == TOP)
    def _():
        span = span_of(TOP)

        def step(n, carry):
            h, i = n // mates, n % mates

            @pl.when(i == 0)
            def _():
                own_await(h)
                kv_await(h, split, split)

            @pl.when((n == 0) & (s == 1))
            def _():
                hand_hub(1, 0, 2)

            turn(HUB, h, i, top_pages, span, TOP, True)

            return carry

        lax.fori_loop(0, per_core * mates, step, 0)

        @pl.when(s == 0)
        def _():
            settle_kv(2 * (pages_here * per_core * sub_size - 1), 1)
            pl.semaphore_signal(go, device_id={"sub": 1}, device_id_type=MESH)

        @pl.when(s == 1)
        def _():
            pl.semaphore_wait(go, 1)
            hand_hub(1, last, 2)

    def finals():
        settle(o_recv.at[0], per_core * mates)

    finals()

    @pl.when(z == HUB)
    def _():
        settle_kv(2 * pages_here * (per_core + 1))
        settle(o_send.at[NEAR], per_core * mates)

        @pl.when(s == 0)
        def _():
            settle(o_send.at[FAR], per_core * mates)

        @pl.when(s == 1)
        def _():
            settle(o_send.at[FAR], last * mates)

    @pl.when(z == TOP)
    def _():
        settle_kv(2 * pages_here * per_core)

        @pl.when(s == 0)
        def _():
            settle_kv(2, 2)

        @pl.when(s == 1)
        def _():
            settle_kv(2 * per_core * sub_size, 1)

    @pl.when(z >= HUB)
    def _():
        settle(q_send.at[1], per_core * (mates - 1))
        settle(o_send.at[HUB], per_core * (mates - 1))

    @pl.when(z == NEAR)
    def _():
        settle(q_send.at[1], per_core * mates)

    @pl.when((z == FAR) & (s == 0))
    def _():
        settle(q_send.at[1], per_core * mates - AHEAD)

    @pl.when((z == FAR) & (s == 1))
    def _():
        settle(q_send.at[1], per_core * mates - 1 - AHEAD)
        settle(o_send.at[FAR], mates - 1)


def served(queries, kv_cache, page_counts):
    ctx_size, sub_size = lax.axis_size("ctx"), lax.axis_size("sub")
    head_size = lax.axis_size("head")
    pages_here = kv_cache.shape[1] // PAGE
    mates = head_size * sub_size
    per_core = KVH // mates
    group = HQ // KVH
    live = pages_here * ctx_size * sub_size // 2
    tok_rows = queries.shape[0]
    slots = ctx_size - 1
    dma = pltpu.SemaphoreType.DMA
    chunk = (slots, per_core, mates, tok_rows, group * HD)
    return pl.pallas_call(
        functools.partial(serve_kernel, (head_size, sub_size, pages_here)),
        out_shape=jax.ShapeDtypeStruct(queries.shape, jnp.bfloat16),
        in_specs=[
            pl.BlockSpec(memory_space=pl.ANY),
            pl.BlockSpec(memory_space=pl.ANY),
            pl.BlockSpec(memory_space=pl.ANY),
        ],
        out_specs=pl.BlockSpec(memory_space=pl.ANY),
        scratch_shapes=[
            pltpu.SMEM((REQS,), jnp.int32),
            pltpu.VMEM((per_core, 2, live * PAGE, HD), jnp.bfloat16),
            pltpu.VMEM(chunk, jnp.bfloat16),
            pltpu.VMEM(chunk, jnp.bfloat16),
            pltpu.VMEM((group * tok_rows, (live - 3) * PAGE), jnp.float32),
            pltpu.VMEM((group * tok_rows, (live - 3) * PAGE), jnp.float32),
            dma((1,)),
            dma((2,)),
            dma((slots - 1, per_core, mates)),
            dma((per_core,)),
            dma((slots,)),
            dma((1,)),
            dma((3,)),
            dma((per_core, 3)),
            pltpu.SemaphoreType.REGULAR,
        ],
        compiler_params=pltpu.CompilerParams(
            collective_id=0, has_side_effects=True, vmem_limit_bytes=VMEM_LIMIT
        ),
    )(
        pltpu.with_memory_space_constraint(page_counts, pltpu.HBM),
        pltpu.with_memory_space_constraint(queries, pltpu.HBM),
        pltpu.with_memory_space_constraint(kv_cache, pltpu.HBM),
    )


def solution(mesh):
    specs = dict(
        mesh=mesh,
        in_specs=(
            P(("grp", "ctx", "head", "sub"), None),
            P(None, ("grp", "ctx", "sub"), "head"),
            P("grp"),
        ),
        out_specs=P(("grp", "ctx", "head", "sub"), None),
        check_vma=False,
    )

    def run(queries, kv_cache, page_counts):
        body = served if can_serve(mesh, kv_cache.shape[1]) else per_device
        return jax.shard_map(body, **specs)(queries, kv_cache, page_counts)

    return run
```
